256 devices in a mesh: dp: 32 (over z_hi, x, core), tensor: 8 (over z_lo, y).
Axes of the slice: x: 4, y: 4, z: 8 (z_hi: 4, z_lo: 2; z = z_hi * 2 + z_lo), core: 2. Of those that a mesh axis runs over, the one named last changes fastest.
Arguments:
- tokens: bfloat16 [32768, 2048], P('dp', 'tensor'), may hold values from -6 to 6
- gain: bfloat16 [2048], replicated, may hold values from 0.099609375 to 1.8984375
- gate_weight: bfloat16 [2048, 7168], P(None, 'tensor'), may hold values from -0.125 to 0.125
- up_weight: bfloat16 [2048, 7168], P(None, 'tensor'), may hold values from -0.125 to 0.125
- down_weight: bfloat16 [7168, 2048], P('tensor'), may hold values from -0.0625 to 0.0625
- cotangent: bfloat16 [32768, 2048], P('dp', 'tensor'), may hold values from -6 to 6
- lengths: int32 [64], P('dp'), may hold values from 1 to 512, 8192 in all
Outputs:
- layer_out: bfloat16 [32768, 2048], P('dp', 'tensor')
- input_grad: bfloat16 [32768, 2048], P('dp', 'tensor')
The draws below stay inside these ranges and needn't reach their ends.
Inputs may be any that keep to these rules, and one draw needn't show every extreme that they name: The lengths sum to exactly 8192; at least one sequence has exactly 512 tokens.
All inputs are finite; a program needn't handle non-finite values. No bound on the sum of `lengths` on one device may be relied on, other than what follows from the above.
Results may differ from the reference program's by a relative error of at most 0.015.
Values may be sent and summed in bfloat16 or wider, within the bound.
A program may use at most 128 MiB of HBM per device.

```python
import math
import jax
import jax.numpy as jnp
import numpy as np
from jax import lax

D = 2048
FF = 7168
L = 512
TOK_DEV = 256
SEQS = 64
ROWS = 32768
TOTAL = 8192
N_DP = 32


def steps_of(key, shape, pieces, low, top_value):
    def one(dim, shards_of):
        heights = jax.random.uniform(jax.random.fold_in(jax.random.fold_in(key, 6), dim), (shards_of,), jnp.float32, low / len(pieces), top_value / len(pieces))
        return jnp.repeat(jnp.exp(heights), shape[dim] // shards_of).reshape((-1,) + (1,) * (len(shape) - dim - 1))

    loudness = one(*pieces[0])
    for cut in pieces[1:]:
        loudness = loudness * one(*cut)
    return loudness


def split_up(number_of, total, reach, lean):
    loads = [(1 << 20) // math.isqrt(grade ** lean) + 1 for grade in range(2, number_of + 1)]
    rest, given = total - reach - (number_of - 1), [1] * (number_of - 1)
    while rest > 0:
        free = [i for i in range(number_of - 1) if given[i] < reach]
        whole, left = sum([loads[i] for i in free]), rest
        for i in free:
            addition = min(reach - given[i], max(1, left * loads[i] // whole), rest)
            given[i] = given[i] + addition
            rest = rest - addition
    return np.array([reach] + given)


def ragged_sizes(rng, amount, total, reach, lean):
    if amount == 2:
        one = jax.random.randint(rng, (), max(1, total - reach), min(reach, total - 1) + 1)
        return jnp.stack([one, total - one])
    tallies = jnp.asarray(split_up(amount, total, reach, lean), jnp.int32)
    couples = (amount - 1) // 2
    donor, sink = tallies[1:1 + 2 * couples:2], tallies[2:2 + 2 * couples:2]
    slack = jnp.minimum(donor - 1, reach - sink)
    passed = jax.random.randint(jax.random.fold_in(rng, 1), (couples,), 0, 1 << 20) % (slack + 1)
    tallies = tallies.at[1:1 + 2 * couples:2].set(donor - passed).at[2:2 + 2 * couples:2].set(sink + passed)
    return tallies[jax.random.permutation(jax.random.fold_in(rng, 2), amount)]


def noise(rng, extent, width, most, pieces=(), held_as=jnp.bfloat16):
    level = steps_of(rng, extent, pieces, -0.22, 0.18) if pieces else 1.0
    drawn = jax.random.normal(rng, extent, jnp.float32) * width * level
    return jnp.minimum(jnp.maximum(drawn, -most), most).astype(held_as)


def setup_inputs(seed: int = 0) -> dict:
    key_list = jax.random.split(jax.random.key(seed), 8)
    return {
        "tokens": noise(key_list[0], (ROWS, D), 1.0, 6.0, ((0, 32), (1, 8))),
        "gain": jnp.clip(1.0 + 0.18 * jax.random.normal(key_list[1], (D,), jnp.float32), 0.099609375, 1.8984375).astype(jnp.bfloat16),
        "gate_weight": noise(key_list[2], (D, FF), D ** -0.5, 0.125, ((1, 8),)),
        "up_weight": noise(key_list[3], (D, FF), D ** -0.5, 0.125, ((1, 8),)),
        "down_weight": noise(key_list[4], (FF, D), FF ** -0.5, 0.0625, ((0, 8),)),
        "cotangent": noise(key_list[5], (ROWS, D), 1.0, 6.0, ((0, 32), (1, 8))),
        "lengths": ragged_sizes(key_list[6], SEQS, TOTAL, L, 2).astype(jnp.int32),
    }


EPSILON = 1e-05

def layer_block(inputs, cotan_rows, gain, gate_weight, up_weight, down_weight):
    xfloat = inputs.astype(jnp.float32)
    scaler = lax.rsqrt(lax.optimization_barrier(jnp.mean(xfloat * xfloat, axis=1, keepdims=True)) + EPSILON)
    unit_rows = xfloat * scaler
    gain_float = gain.astype(jnp.float32)
    normed = (unit_rows * gain_float).astype(jnp.bfloat16)
    gate_values = jnp.dot(normed, gate_weight, preferred_element_type=jnp.float32)
    up_values = jnp.dot(normed, up_weight, preferred_element_type=jnp.float32)
    sigmoid = jax.nn.sigmoid(gate_values)
    activation = gate_values * sigmoid
    hidden = (activation * up_values).astype(jnp.bfloat16)
    layer_sum = jnp.dot(hidden, down_weight, preferred_element_type=jnp.float32)
    block_out = (xfloat + layer_sum).astype(jnp.bfloat16)
    hidden_grad = jnp.dot(cotan_rows, down_weight.T, preferred_element_type=jnp.float32)
    gate_grad = (hidden_grad * up_values * sigmoid * (1.0 + gate_values * (1.0 - sigmoid))).astype(jnp.bfloat16)
    up_grad = (hidden_grad * activation).astype(jnp.bfloat16)
    normed_grad = jnp.dot(gate_grad, gate_weight.T, preferred_element_type=jnp.float32) + jnp.dot(up_grad, up_weight.T, preferred_element_type=jnp.float32)
    unit_grad = normed_grad * gain_float
    inner_mean = lax.optimization_barrier(jnp.mean(unit_grad * unit_rows, axis=1, keepdims=True))
    block_grad = (cotan_rows.astype(jnp.float32) + scaler * (unit_grad - unit_rows * inner_mean)).astype(jnp.bfloat16)
    return (block_out, block_grad)

def reference(tokens, gain, gate_weight, up_weight, down_weight, cotangent, lengths):
    total_rows = tokens.shape[0]
    row_ids = jnp.arange(total_rows, dtype=jnp.int32)
    is_valid = row_ids % L < lengths[row_ids // L]
    chosen = jnp.nonzero(is_valid, size=TOTAL)[0].astype(jnp.int32)
    picked = jnp.take(tokens, chosen, axis=0).reshape(N_DP, TOK_DEV, D)
    cotan_picked = jnp.take(cotangent, chosen, axis=0).reshape(N_DP, TOK_DEV, D)

    def per_block(block_args):
        return layer_block(block_args[0], block_args[1], gain, gate_weight, up_weight, down_weight)
    block_out, block_grad = lax.map(per_block, (picked, cotan_picked))
    layer_out = jnp.zeros_like(tokens).at[chosen].set(block_out.reshape(TOTAL, D))
    input_grad = jnp.zeros_like(tokens).at[chosen].set(block_grad.reshape(TOTAL, D))
    return (layer_out, input_grad)
```

```python
import functools

import jax
import jax.numpy as jnp
from jax import lax
from jax.experimental import pallas as pl
from jax.experimental.pallas import tpu as pltpu
from jax.sharding import PartitionSpec as P

TOK_DEV = 256
EPSILON = 1e-05
GROUP = 8
TILE = 8
CAPACITIES = (320, 352, 384, 448, 512)
MESH = pl.DeviceIdType.MESH
NT = (((1,), (1,)), ((), ()))


def remote(src, dst, send_sem, recv_sem, dp, tensor):
    return pltpu.make_async_remote_copy(
        src_ref=src, dst_ref=dst, send_sem=send_sem, recv_sem=recv_sem,
        device_id=(dp, tensor), device_id_type=MESH,
    )


def signal(sem, dp, tensor):
    pl.semaphore_signal(sem, inc=1, device_id=(dp, tensor), device_id_type=MESH)


def exchange_kernel(
    members, tok_ref, cot_ref, len_ref, tok_out, cot_out, len_out,
    local_sem, send_sem, recv_sem, len_send, len_recv,
):
    dp = lax.axis_index("dp")
    tensor = lax.axis_index("tensor")
    base = dp // GROUP * GROUP
    own = dp % GROUP
    barrier = pltpu.get_barrier_semaphore()

    def greet(step, carry):
        signal(barrier, (dp + step) % members, tensor)
        return carry

    lax.fori_loop(1, members, greet, 0)
    local = [
        pltpu.make_async_copy(source.at[:, :, 0], target.at[0], local_sem.at[i])
        for i, (source, target) in enumerate(((tok_ref, tok_out), (cot_ref, cot_out)))
    ]
    for copy in local:
        copy.start()
    keep = pltpu.make_async_copy(len_ref, len_out.at[dp], local_sem.at[2])
    keep.start()
    pl.semaphore_wait(barrier, members - 1)

    def len_copy(step):
        return remote(
            len_ref, len_out.at[dp], len_send.at[step - 1], len_recv.at[step - 1],
            (dp + step) % members, tensor,
        )

    def share(step, carry):
        len_copy(step).start()
        return carry

    lax.fori_loop(1, members, share, 0)
    copies = []
    for i, (source, target) in enumerate(((tok_ref, tok_out), (cot_ref, cot_out))):
        for k in range(1, GROUP):
            copies.append(
                remote(
                    source.at[:, :, k], target.at[k], send_sem.at[i, k], recv_sem.at[i, k],
                    base + (own + k) % GROUP, tensor,
                )
            )
    for copy in copies:
        copy.start()

    def collect(step, carry):
        len_copy(step).wait()
        return carry

    lax.fori_loop(1, members, collect, 0)
    for copy in local:
        copy.wait()
    keep.wait()
    for copy in copies:
        copy.wait()


def exchange(tokens, cotangent, lengths, members):
    seqs = lengths.shape[0]
    rows, width = tokens.shape
    rounds = rows // (seqs * GROUP * TILE)
    shape = (seqs, rounds, GROUP, TILE, width)
    slots = jax.ShapeDtypeStruct((GROUP, seqs, rounds, TILE, width), tokens.dtype)
    padded = jnp.pad(lengths, (0, 128 - seqs)).reshape(1, 128)
    anywhere = pl.BlockSpec(memory_space=pl.ANY)
    tok, cot, lens = pl.pallas_call(
        functools.partial(exchange_kernel, members),
        out_shape=(slots, slots, jax.ShapeDtypeStruct((members, 1, 128), jnp.int32)),
        in_specs=[anywhere, anywhere, pl.BlockSpec(memory_space=pltpu.VMEM)],
        out_specs=(anywhere, anywhere, pl.BlockSpec(memory_space=pltpu.VMEM)),
        scratch_shapes=[
            pltpu.SemaphoreType.DMA((3,)),
            pltpu.SemaphoreType.DMA((2, GROUP)),
            pltpu.SemaphoreType.DMA((2, GROUP)),
            pltpu.SemaphoreType.DMA((members - 1,)),
            pltpu.SemaphoreType.DMA((members - 1,)),
        ],
        compiler_params=pltpu.CompilerParams(collective_id=0, has_side_effects=True),
        name="exchange",
    )(tokens.reshape(shape), cotangent.reshape(shape), padded)
    return tok.reshape(rows, width), cot.reshape(rows, width), lens[:, 0, :seqs]


def tile_count(length, k):
    cycle = GROUP * TILE
    return length // cycle * TILE + jnp.clip(length % cycle - TILE * k, 0, TILE)


def layer_kernel(
    cap, seqs, rounds,
    lens_ref, tok_slots, cot_slots, gain_ref, wg_ref, wu_ref, wd_ref,
    layer_ref, grad_ref,
    wgu, wd, tokf, cotf, hidden, act, dact, both, ggug, scale_ref, mean_ref,
    layer_send, layer_recv, grad_send, grad_recv, layer_back, grad_back,
    w_sem, ag_send, ag_recv, rs_send, rs_recv, out_send, out_recv,
):
    f32, bf16 = jnp.float32, jnp.bfloat16
    dp = lax.axis_index("dp")
    tensor = lax.axis_index("tensor")
    base = dp // GROUP * GROUP
    own = dp % GROUP
    width = tok_slots.shape[1]
    parts = tokf.shape[1] // width
    units = hidden.shape[1]
    seg = rounds * TILE

    pieces = units // 128
    w_copies = []
    for j in range(pieces):
        for i, source in enumerate((wg_ref, wu_ref)):
            w_copies.append(
                pltpu.make_async_copy(
                    source.at[:, pl.ds(j * 128, 128)],
                    wgu.at[:, pl.ds(j * 256 + i * 128, 128)],
                    w_sem.at[2 * j + i],
                )
            )
    w_copies.append(pltpu.make_async_copy(wd_ref, wd, w_sem.at[2 * pieces]))
    for copy in w_copies:
        copy.start()
    barrier = pltpu.get_barrier_semaphore()
    for k in range(1, parts):
        signal(barrier, dp, tensor ^ k)
    for k in range(1, GROUP):
        signal(barrier, base + (own + k) % GROUP, tensor)

    counts, starts, total = [], [], jnp.int32(0)
    for k in range(GROUP):
        home = base + (own - k + GROUP) % GROUP
        for s in range(seqs):
            count = tile_count(lens_ref[home * seqs + s], k)
            counts.append(count)
            starts.append(total)
            total = total + count
    slot_rows = GROUP * seqs * seg
    lane = lax.broadcasted_iota(jnp.int32, (1, slot_rows), 1)
    place = jnp.full((1, slot_rows), -1, jnp.int32)
    for i in range(GROUP * seqs):
        inside = lane - i * seg
        place = jnp.where((inside >= 0) & (inside < counts[i]), inside + starts[i], place)
    row = lax.broadcasted_iota(jnp.int32, (cap, slot_rows), 0)
    picks = jnp.where(row == place, 1.0, 0.0).astype(bf16)
    block = pl.ds(pl.multiple_of(tensor * width, width), width)
    tokf[:, block] = jnp.dot(picks, tok_slots[...], preferred_element_type=f32).astype(bf16)
    cotf[:, block] = jnp.dot(picks, cot_slots[...], preferred_element_type=f32).astype(bf16)
    pl.semaphore_wait(barrier, parts + GROUP - 2)

    gathers = []
    for i, full in enumerate((tokf, cotf)):
        mine = []
        for k in range(1, parts):
            mine.append(
                remote(
                    full.at[:, block], full.at[:, block], ag_send.at[i, k], ag_recv.at[i, k],
                    dp, tensor ^ k,
                )
            )
        for copy in mine:
            copy.start()
        gathers.append(mine)
    for copy in gathers[0]:
        copy.wait_recv()

    def square(b, total):
        x = tokf[:, pl.ds(pl.multiple_of(b * width, width), width)].astype(f32)
        return total + jnp.sum(x * x, axis=1, keepdims=True)

    total_sq = lax.fori_loop(0, parts, square, jnp.zeros((cap, 1), f32))
    scaler = lax.rsqrt(total_sq * (1.0 / (parts * width)) + EPSILON)
    scale_ref[...] = jnp.broadcast_to(scaler, (cap, 128))
    normed = ggug

    def norm(b, carry):
        at = pl.ds(pl.multiple_of(b * width, width), width)
        x = tokf[:, at].astype(f32)
        normed[:, at] = (x * scale_ref[:, :1] * gain_ref[:, at].astype(f32)).astype(bf16)
        return carry

    lax.fori_loop(0, parts, norm, 0)
    for copy in w_copies:
        copy.wait()

    def forward(j, carry):
        at = pl.ds(pl.multiple_of(j * 128, 128), 128)
        gu = jnp.dot(
            normed[:, : parts * width], wgu[:, pl.ds(pl.multiple_of(j * 256, 256), 256)],
            preferred_element_type=f32,
        )
        gate, up = gu[:, :128], gu[:, 128:]
        sigmoid = jax.nn.sigmoid(gate)
        silu = gate * sigmoid
        slope = up * sigmoid * (1.0 + gate * (1.0 - sigmoid))
        hidden[:, at] = (silu * up).astype(bf16)
        act[:, at] = silu
        dact[:, at] = slope
        both[:, at] = slope * gate + silu * up
        return carry

    lax.fori_loop(0, pieces, forward, 0)

    def layer_part(k):
        at = pl.ds(pl.multiple_of((tensor ^ k) * width, width), width)
        return jnp.dot(hidden[...], wd[:, at], preferred_element_type=f32).astype(bf16)

    def rs_copy(i, k, send, recv):
        return remote(
            send.at[k], recv.at[k], rs_send.at[i, k], rs_recv.at[i, k], dp, tensor ^ k
        )

    def layer_step(k, carry):
        layer_send[k] = layer_part(k)
        rs_copy(0, k, layer_send, layer_recv).start()
        return carry

    lax.fori_loop(1, parts, layer_step, 0)
    layer_send[0] = layer_part(0)

    for copy in gathers[1]:
        copy.wait_recv()

    mean_ref[...] = jnp.zeros_like(mean_ref)

    def backward(j, carry):
        at = pl.ds(pl.multiple_of(j * 128, 128), 128)
        hgrad = lax.dot_general(cotf[...], wd[at, :], NT, preferred_element_type=f32)
        ggug[:, pl.ds(pl.multiple_of(j * 256, 256), 128)] = (hgrad * dact[:, at]).astype(bf16)
        ggug[:, pl.ds(pl.multiple_of(j * 256 + 128, 128), 128)] = (hgrad * act[:, at]).astype(bf16)
        mean_ref[...] += hgrad * both[:, at]
        return carry

    lax.fori_loop(0, pieces, backward, 0)
    mean = jnp.sum(mean_ref[...], axis=1, keepdims=True) * (1.0 / (parts * width))
    mean_ref[...] = jnp.broadcast_to(mean * scale_ref[:, :1], (cap, 128))

    def grad_part(k):
        at = pl.ds(pl.multiple_of((tensor ^ k) * width, width), width)
        terms = lax.dot_general(
            ggug[:, : 2 * units], wgu[at, :], NT, preferred_element_type=f32
        )
        unit_part = tokf[:, at].astype(f32) * mean_ref[:, :1]
        return (scale_ref[:, :1] * (terms * gain_ref[:, at].astype(f32) - unit_part)).astype(bf16)

    def grad_step(k, carry):
        grad_send[k] = grad_part(k)
        rs_copy(1, k, grad_send, grad_recv).start()
        return carry

    lax.fori_loop(1, parts, grad_step, 0)
    grad_send[0] = grad_part(0)

    def finish(i, full, send, recv, back, out):
        for k in range(1, parts):
            rs_copy(i, k, send, recv).wait_recv()
        result = full[:, block].astype(f32) + send[0].astype(f32)
        for k in range(1, parts):
            result = result + recv[k].astype(f32)
        result = result.astype(bf16)
        copies = []
        for k in list(range(1, GROUP)) + [0]:
            inside = lax.broadcasted_iota(jnp.int32, (seqs * seg, 1), 0)
            here = jnp.full((seqs * seg, 1), -1, jnp.int32)
            for s in range(seqs):
                at = inside - s * seg
                here = jnp.where(
                    (at >= 0) & (at < counts[k * seqs + s]), at + starts[k * seqs + s], here
                )
            column = lax.broadcasted_iota(jnp.int32, (seqs * seg, cap), 1)
            spread = jnp.where(column == here, 1.0, 0.0).astype(bf16)
            rows = jnp.dot(spread, result, preferred_element_type=f32)
            back[k] = rows.reshape(seqs, rounds, TILE, width).astype(bf16)
            if k:
                copy = remote(
                    back.at[k], out.at[:, :, k], out_send.at[i, k], out_recv.at[i, k],
                    base + (own - k + GROUP) % GROUP, tensor,
                )
            else:
                copy = pltpu.make_async_copy(back.at[0], out.at[:, :, 0], out_send.at[i, 0])
            copy.start()
            copies.append(copy)
        return copies

    copies = finish(0, tokf, layer_send, layer_recv, layer_back, layer_ref)
    copies += finish(1, cotf, grad_send, grad_recv, grad_back, grad_ref)
    for mine in gathers:
        for copy in mine:
            copy.wait_send()
    for i, (send, recv) in enumerate(((layer_send, layer_recv), (grad_send, grad_recv))):
        for k in range(1, parts):
            rs_copy(i, k, send, recv).wait_send()
    for copy in copies:
        copy.wait()


def layer(cap, number, lens, tok, cot, gain, gate_weight, up_weight, down_weight):
    rows, width = tok.shape
    units, features = down_weight.shape
    parts = features // width
    seqs = lens.shape[1]
    rounds = rows // (seqs * GROUP * TILE)
    f32, bf16 = jnp.float32, jnp.bfloat16
    out = jax.ShapeDtypeStruct((seqs, rounds, GROUP, TILE, width), bf16)
    anywhere = pl.BlockSpec(memory_space=pl.ANY)
    vmem = pl.BlockSpec(memory_space=pltpu.VMEM)
    exchange_buffer = pltpu.VMEM((parts, cap, width), bf16)
    back_buffer = pltpu.VMEM((GROUP, seqs, rounds, TILE, width), bf16)
    layer_out, input_grad = pl.pallas_call(
        functools.partial(layer_kernel, cap, seqs, rounds),
        out_shape=(out, out),
        in_specs=[pl.BlockSpec(memory_space=pltpu.SMEM), vmem, vmem, vmem]
        + [anywhere] * 3,
        out_specs=(anywhere, anywhere),
        scratch_shapes=[
            pltpu.VMEM((features, 2 * units), bf16),
            pltpu.VMEM((units, features), bf16),
            pltpu.VMEM((cap, features), bf16),
            pltpu.VMEM((cap, features), bf16),
            pltpu.VMEM((cap, units), bf16),
            pltpu.VMEM((cap, units), f32),
            pltpu.VMEM((cap, units), f32),
            pltpu.VMEM((cap, units), f32),
            pltpu.VMEM((cap, max(features, 2 * units)), bf16),
            pltpu.VMEM((cap, 128), f32),
            pltpu.VMEM((cap, 128), f32),
            exchange_buffer, exchange_buffer, exchange_buffer, exchange_buffer,
            back_buffer, back_buffer,
            pltpu.SemaphoreType.DMA((2 * (units // 128) + 1,)),
            pltpu.SemaphoreType.DMA((2, parts)),
            pltpu.SemaphoreType.DMA((2, parts)),
            pltpu.SemaphoreType.DMA((2, parts)),
            pltpu.SemaphoreType.DMA((2, parts)),
            pltpu.SemaphoreType.DMA((2, GROUP)),
            pltpu.SemaphoreType.DMA((2, GROUP)),
        ],
        compiler_params=pltpu.CompilerParams(
            collective_id=number, has_side_effects=True, vmem_limit_bytes=58 << 20
        ),
        name=f"layer_{cap}",
    )(lens.reshape(-1), tok, cot, gain.reshape(1, -1), gate_weight, up_weight, down_weight)
    return layer_out.reshape(rows, width), input_grad.reshape(rows, width)


def largest_load(lens):
    planes = lens.reshape(-1, GROUP, lens.shape[1])
    member = jnp.arange(GROUP, dtype=jnp.int32)
    phase = (member[:, None] - member[None, :]) % GROUP
    count = tile_count(planes[:, None], phase[None, :, :, None])
    return jnp.max(jnp.sum(count, axis=(2, 3)))


def shards(tokens, gain, gate_weight, up_weight, down_weight, cotangent, lengths):
    members = lax.axis_size("dp")
    tok, cot, lens = exchange(tokens, cotangent, lengths, members)
    load = largest_load(lens)
    choice = jnp.sum((load > jnp.array(CAPACITIES, jnp.int32)).astype(jnp.int32))

    def sized(number, cap):
        return lambda: layer(
            cap, number, lens, tok, cot, gain, gate_weight, up_weight, down_weight
        )

    branches = [sized(i + 1, cap) for i, cap in enumerate(CAPACITIES)]
    branches.append(
        lambda: spread_evenly(
            tokens, gain, gate_weight, up_weight, down_weight, cotangent, lengths
        )
    )
    return lax.switch(choice, branches)


def lookup_small(index_values, table):
    picks = index_values[..., None] == jnp.arange(table.shape[0], dtype=jnp.int32)
    return jnp.sum(jnp.where(picks, table, 0), axis=-1)


def count_below(values, bounds):
    return jnp.sum((values[..., None] >= bounds).astype(jnp.int32), axis=-1)


def layer_core(token_part, cotan_part, gain, gate_weight, up_weight, down_weight):
    width_part = token_part.shape[1]
    lane_index = lax.axis_index("tensor")
    token_full, cotan_full = (
        lax.all_gather(token_part, "tensor", axis=1, tiled=True),
        lax.all_gather(cotan_part, "tensor", axis=1, tiled=True),
    )
    xfloat = token_full.astype(jnp.float32)
    scaler = lax.rsqrt(jnp.mean(xfloat * xfloat, axis=1, keepdims=True) + EPSILON)
    unit_rows = xfloat * scaler
    gain_float = gain.astype(jnp.float32)
    normed = (unit_rows * gain_float).astype(jnp.bfloat16)
    gate_values = jnp.dot(normed, gate_weight, preferred_element_type=jnp.float32)
    up_values = jnp.dot(normed, up_weight, preferred_element_type=jnp.float32)
    sigmoid = jax.nn.sigmoid(gate_values)
    activation = gate_values * sigmoid
    hidden = (activation * up_values).astype(jnp.bfloat16)
    layer_terms = jnp.dot(hidden, down_weight, preferred_element_type=jnp.float32)
    layer_sum = lax.psum_scatter(
        layer_terms.astype(jnp.bfloat16), "tensor", scatter_dimension=1, tiled=True
    ).astype(jnp.float32)
    layer_part = (token_part.astype(jnp.float32) + layer_sum).astype(jnp.bfloat16)
    contract_last = (((1,), (1,)), ((), ()))
    hidden_grad = lax.dot_general(
        cotan_full, down_weight, contract_last, preferred_element_type=jnp.float32
    )
    gate_grad = (hidden_grad * up_values * sigmoid * (1.0 + gate_values * (1.0 - sigmoid))).astype(
        jnp.bfloat16
    )
    up_grad = (hidden_grad * activation).astype(jnp.bfloat16)
    normed_terms = lax.dot_general(
        gate_grad, gate_weight, contract_last, preferred_element_type=jnp.float32
    )
    normed_terms = normed_terms + lax.dot_general(
        up_grad, up_weight, contract_last, preferred_element_type=jnp.float32
    )
    column_start = lane_index * width_part
    normed_grad = lax.psum(normed_terms, "tensor")
    unit_grad = normed_grad * gain_float
    inner_mean = jnp.mean(unit_grad * unit_rows, axis=1, keepdims=True)
    full_grad = scaler * (unit_grad - unit_rows * inner_mean)
    part_grad = lax.dynamic_slice_in_dim(full_grad, column_start, width_part, 1)
    grad_part = (cotan_part.astype(jnp.float32) + part_grad).astype(jnp.bfloat16)
    return (layer_part, grad_part)


def spread_evenly(tokens, gain, gate_weight, up_weight, down_weight, cotangent, lengths):
    row_total, width_part = tokens.shape
    seq_count = lengths.shape[0]
    seq_length = row_total // seq_count
    row_ids = jnp.arange(row_total, dtype=jnp.int32)
    row_seq = row_ids // seq_length
    row_pos = row_ids % seq_length
    row_limit = lookup_small(row_seq, lengths)
    is_valid = row_pos < row_limit
    members = lax.axis_size("dp")
    my_index = lax.axis_index("dp")
    own_count = jnp.sum(lengths)
    all_counts = lax.all_gather(own_count.reshape(1), "dp", axis=0, tiled=True)
    count_ends = jnp.cumsum(all_counts)
    count_starts = count_ends - all_counts
    own_start = lookup_small(my_index, count_starts)
    slot_count = (row_total + members - 2) // members + 1
    seq_ends = jnp.cumsum(lengths)
    seq_starts = seq_ends - lengths
    peer_ids = jnp.arange(members, dtype=jnp.int32)[:, None]
    slot_ids = jnp.arange(slot_count, dtype=jnp.int32)[None, :]
    global_rank = (own_start // members + slot_ids) * members + peer_ids
    local_rank = global_rank - own_start
    is_sent = (local_rank >= 0) & (local_rank < own_count)
    local_safe = jnp.where(is_sent, local_rank, 0)
    send_seq = count_below(local_safe, seq_ends)
    send_row = send_seq * seq_length + local_safe - lookup_small(send_seq, seq_starts)
    flat_rows = send_row.reshape(-1)

    def pack_rows(source):
        picked = jnp.take(source, flat_rows, axis=0).reshape(members, slot_count, width_part)
        return jnp.where(is_sent[:, :, None], picked, jnp.zeros_like(picked))

    got_tokens, got_cotan = (
        lax.all_to_all(pack_rows(tokens), "dp", split_axis=0, concat_axis=0, tiled=True),
        lax.all_to_all(pack_rows(cotangent), "dp", split_axis=0, concat_axis=0, tiled=True),
    )
    packed_ids = jnp.arange(TOK_DEV, dtype=jnp.int32)
    packed_rank = packed_ids * members + my_index
    source_ids = count_below(packed_rank, count_ends)
    source_start = lookup_small(source_ids, count_starts)
    recv_flat = source_ids * slot_count + packed_ids - source_start // members
    token_packed = jnp.take(got_tokens.reshape(members * slot_count, width_part), recv_flat, axis=0)
    cotan_packed = jnp.take(got_cotan.reshape(members * slot_count, width_part), recv_flat, axis=0)
    layer_packed, grad_packed = layer_core(
        token_packed, cotan_packed, gain, gate_weight, up_weight, down_weight
    )

    def unpack_slots(values):
        empty = jnp.zeros((members * slot_count, width_part), values.dtype)
        return empty.at[recv_flat].set(values).reshape(members, slot_count, width_part)

    back_layer, back_grad = (
        lax.all_to_all(unpack_slots(layer_packed), "dp", split_axis=0, concat_axis=0, tiled=True),
        lax.all_to_all(unpack_slots(grad_packed), "dp", split_axis=0, concat_axis=0, tiled=True),
    )
    row_rank = own_start + lookup_small(row_seq, seq_starts) + row_pos
    back_flat = row_rank % members * slot_count + row_rank // members - own_start // members
    back_flat = jnp.where(is_valid, back_flat, 0)
    layer_rows = jnp.take(back_layer.reshape(members * slot_count, width_part), back_flat, axis=0)
    grad_rows = jnp.take(back_grad.reshape(members * slot_count, width_part), back_flat, axis=0)
    zero_rows = jnp.zeros_like(tokens)
    layer_out = jnp.where(is_valid[:, None], layer_rows, zero_rows)
    input_grad = jnp.where(is_valid[:, None], grad_rows, zero_rows)
    return (layer_out, input_grad)


def solution(mesh):
    placed = (
        P("dp", "tensor"),
        P(),
        P(None, "tensor"),
        P(None, "tensor"),
        P("tensor", None),
        P("dp", "tensor"),
        P("dp"),
    )
    return jax.shard_map(
        shards,
        mesh=mesh,
        in_specs=placed,
        out_specs=(P("dp", "tensor"), P("dp", "tensor")),
        check_vma=False,
    )
```

```python
import functools

import jax
import jax.numpy as jnp
from jax import lax
from jax.experimental import pallas as pl
from jax.experimental.pallas import tpu as pltpu
from jax.sharding import PartitionSpec as P

EPSILON = 1e-05
GROUP = 8
TILE = 8
CAPACITIES = (320, 352, 384, 448, 1024)
MESH = pl.DeviceIdType.MESH
NT = (((1,), (1,)), ((), ()))
f32, bf16, i32 = jnp.float32, jnp.bfloat16, jnp.int32


def remote(src, dst, send_sem, recv_sem, dp, tensor):
    return pltpu.make_async_remote_copy(
        src_ref=src, dst_ref=dst, send_sem=send_sem, recv_sem=recv_sem,
        device_id=(dp, tensor), device_id_type=MESH,
    )


def signal(sem, dp, tensor):
    pl.semaphore_signal(sem, inc=1, device_id=(dp, tensor), device_id_type=MESH)


def tile_count(length, k):
    cycle = GROUP * TILE
    return length // cycle * TILE + jnp.clip(length % cycle - TILE * k, 0, TILE)


def exchange_kernel(
    members, tok_ref, info_ref, tok_out, info_out, choice_ref,
    local_sem, send_sem, recv_sem, info_send, info_recv,
):
    dp = lax.axis_index("dp")
    tensor = lax.axis_index("tensor")
    base = dp // GROUP * GROUP
    own = dp % GROUP
    barrier = pltpu.get_barrier_semaphore()

    def greet(step, carry):
        signal(barrier, (dp + step) % members, tensor)
        return carry

    lax.fori_loop(1, members, greet, 0)
    local = pltpu.make_async_copy(tok_ref.at[:, :, 0], tok_out.at[0], local_sem.at[0])
    local.start()
    info_out[dp] = info_ref[...]
    pl.semaphore_wait(barrier, members - 1)

    def info_copy(step):
        return remote(
            info_ref, info_out.at[dp], info_send.at[step - 1], info_recv.at[step - 1],
            (dp + step) % members, tensor,
        )

    def share(step, carry):
        info_copy(step).start()
        return carry

    copies = [
        remote(
            tok_ref.at[:, :, k], tok_out.at[k], send_sem.at[k], recv_sem.at[k],
            base + (own + k) % GROUP, tensor,
        )
        for k in range(1, GROUP)
    ]
    for copy in copies:
        copy.start()
    lax.fori_loop(1, members, share, 0)

    def collect(step, carry):
        info_copy(step).wait()
        return carry

    lax.fori_loop(1, members, collect, 0)
    load = jnp.zeros((1, 128), i32)
    for plane in range(members // GROUP):
        held = info_out[plane * GROUP]
        for h in range(1, GROUP):
            held = held + info_out[plane * GROUP + h]
        load = jnp.maximum(load, held)
    lane = lax.broadcasted_iota(i32, (1, 128), 1)
    most = jnp.max(jnp.where(lane < GROUP, load, 0))
    choice = jnp.int32(0)
    for cap in CAPACITIES[:-1]:
        choice = choice + (most > cap).astype(i32)
    choice_ref[0] = choice
    local.wait()
    for copy in copies:
        copy.wait()


def exchange(tokens, lengths, members):
    seqs = lengths.shape[0]
    rows, width = tokens.shape
    rounds = rows // (seqs * GROUP * TILE)
    slots = jax.ShapeDtypeStruct((GROUP, seqs, rounds, TILE, width), tokens.dtype)
    lane = jnp.arange(128, dtype=i32)
    phase = (lane - lax.axis_index("dp")) % GROUP
    info = jnp.where(lane < GROUP, jnp.sum(tile_count(lengths[:, None], phase), axis=0), 0)
    for s in range(seqs):
        info = jnp.where(lane == GROUP + s, lengths[s], info)
    anywhere = pl.BlockSpec(memory_space=pl.ANY)
    vmem = pl.BlockSpec(memory_space=pltpu.VMEM)
    tok, shared, choice = pl.pallas_call(
        functools.partial(exchange_kernel, members),
        out_shape=(
            slots, jax.ShapeDtypeStruct((members, 1, 128), i32), jax.ShapeDtypeStruct((1,), i32)
        ),
        in_specs=[anywhere, vmem],
        out_specs=(anywhere, vmem, pl.BlockSpec(memory_space=pltpu.SMEM)),
        scratch_shapes=[
            pltpu.SemaphoreType.DMA((1,)),
            pltpu.SemaphoreType.DMA((GROUP,)),
            pltpu.SemaphoreType.DMA((GROUP,)),
            pltpu.SemaphoreType.DMA((members - 1,)),
            pltpu.SemaphoreType.DMA((members - 1,)),
        ],
        compiler_params=pltpu.CompilerParams(collective_id=0, has_side_effects=True),
        name="exchange",
    )(tokens.reshape(seqs, rounds, GROUP, TILE, width), info.reshape(1, 128))
    return tok.reshape(rows, width), shared, choice[0]


def layer_kernel(
    cap, split, seqs, rounds,
    info_ref, tok_slots, gain_ref, cot_ref, wg_ref, wu_ref, wd_ref,
    layer_ref, grad_ref,
    wgu, wd, cot_slots, tokf, cotf, hidden, act, dact, both, ggug, scale_ref, mean_ref,
    layer_send, layer_recv, grad_send, grad_recv, layer_back, grad_back,
    w_sem, in_send, in_recv, ag_send, ag_recv, rs_send, rs_recv, out_send, out_recv,
):
    dp = lax.axis_index("dp")
    tensor = lax.axis_index("tensor")
    base = dp // GROUP * GROUP
    own = dp % GROUP
    width = tok_slots.shape[1]
    parts = tokf.shape[1] // width
    units = hidden.shape[1]
    seg = rounds * TILE
    early, late = pl.ds(0, split), pl.ds(split, cap - split)

    pieces = units // 128
    w_copies = []
    for j in range(pieces):
        for i, source in enumerate((wg_ref, wu_ref)):
            w_copies.append(
                pltpu.make_async_copy(
                    source.at[:, pl.ds(j * 128, 128)],
                    wgu.at[:, pl.ds(j * 256 + i * 128, 128)],
                    w_sem.at[2 * j + i],
                )
            )
    w_copies.append(pltpu.make_async_copy(wd_ref, wd, w_sem.at[2 * pieces]))
    barrier = pltpu.get_barrier_semaphore()
    for k in range(1, 5):
        signal(barrier, dp, tensor ^ k)
    for k in range(1, GROUP):
        signal(barrier, base + (own + k) % GROUP, tensor)
    cot_in = [pltpu.make_async_copy(cot_ref.at[:, :, 0], cot_slots.at[0], in_send.at[0])]
    for k in range(1, GROUP):
        cot_in.append(
            remote(
                cot_ref.at[:, :, k], cot_slots.at[k], in_send.at[k], in_recv.at[k],
                base + (own + k) % GROUP, tensor,
            )
        )
    cot_in[0].start()

    counts, starts, total = [], [], jnp.int32(0)
    for k in range(GROUP):
        home = base + (own - k + GROUP) % GROUP
        for s in range(seqs):
            count = tile_count(info_ref[home, 0, GROUP + s], k)
            counts.append(count)
            starts.append(total)
            total = total + count
    slot_rows = GROUP * seqs * seg
    lane = lax.broadcasted_iota(i32, (1, slot_rows), 1)
    place = jnp.full((1, slot_rows), -1, i32)
    for i in range(GROUP * seqs):
        inside = lane - i * seg
        place = jnp.where((inside >= 0) & (inside < counts[i]), inside + starts[i], place)

    def compact(slots):
        row = lax.broadcasted_iota(i32, (cap, slot_rows), 0)
        picks = jnp.where(row == place, 1.0, 0.0).astype(bf16)
        return jnp.dot(picks, slots, preferred_element_type=f32).astype(bf16)

    def at(k):
        return pl.ds(pl.multiple_of((tensor ^ k) * width, width), width)

    tokf[:, at(0)] = compact(tok_slots[...])
    pl.semaphore_wait(barrier, 4 + GROUP - 1)

    def first_hop(i, full):
        return [
            remote(
                full.at[:, at(0)], full.at[:, at(0)], ag_send.at[i, k], ag_recv.at[i, k],
                dp, tensor ^ k,
            )
            for k in (4, 1, 3, 2)
        ]

    def second_hop(i, full):
        to_y = [
            remote(
                full.at[early, at(4)], full.at[early, at(4)],
                ag_send.at[i, 4 + k], ag_recv.at[i, 4 + k], dp, tensor ^ k,
            )
            for k in (1, 3, 2)
        ]
        to_z = [
            remote(
                full.at[late, at(k)], full.at[late, at(k)],
                ag_send.at[i, 7 + k], ag_recv.at[i, 7 + k], dp, tensor ^ 4,
            )
            for k in (1, 3, 2)
        ]
        return to_y, to_z

    def pass_on(first, second):
        to_y, to_z = second
        first[0].wait_recv()
        for copy in to_y:
            copy.start()
        for arrived, copy in zip(first[1:], to_z):
            arrived.wait_recv()
            copy.start()

    tok_first, tok_second = first_hop(0, tokf), second_hop(0, tokf)
    cot_first, cot_second = first_hop(1, cotf), second_hop(1, cotf)
    for copy in tok_first:
        copy.start()
    for copy in cot_in[1:]:
        copy.start()
    for copy in w_copies:
        copy.start()
    pass_on(tok_first, tok_second)
    cot_in[0].wait()
    for copy in cot_in[1:]:
        copy.wait_recv()
    cotf[:, at(0)] = compact(cot_slots[...].reshape(slot_rows, width))
    for copy in tok_second[0] + tok_second[1]:
        copy.wait_recv()
    for copy in cot_first:
        copy.start()

    def square(b, total):
        x = tokf[:, pl.ds(pl.multiple_of(b * width, width), width)].astype(f32)
        return total + jnp.sum(x * x, axis=1, keepdims=True)

    total_sq = lax.fori_loop(0, parts, square, jnp.zeros((cap, 1), f32))
    scaler = lax.rsqrt(total_sq * (1.0 / (parts * width)) + EPSILON)
    scale_ref[...] = jnp.broadcast_to(scaler, (cap, 128))
    normed = ggug

    def norm(b, carry):
        here = pl.ds(pl.multiple_of(b * width, width), width)
        x = tokf[:, here].astype(f32)
        normed[:, here] = (x * scale_ref[:, :1] * gain_ref[:, here].astype(f32)).astype(bf16)
        return carry

    lax.fori_loop(0, parts, norm, 0)
    for copy in w_copies:
        copy.wait()

    def forward(j, carry):
        here = pl.ds(pl.multiple_of(j * 128, 128), 128)
        gu = jnp.dot(
            normed[:, : parts * width], wgu[:, pl.ds(pl.multiple_of(j * 256, 256), 256)],
            preferred_element_type=f32,
        )
        gate, up = gu[:, :128], gu[:, 128:]
        sigmoid = jax.nn.sigmoid(gate)
        silu = gate * sigmoid
        slope = up * sigmoid * (1.0 + gate * (1.0 - sigmoid))
        hidden[:, here] = (silu * up).astype(bf16)
        act[:, here] = silu
        dact[:, here] = slope
        both[:, here] = slope * gate + silu * up
        return carry

    lax.fori_loop(0, pieces, forward, 0)
    pass_on(cot_first, cot_second)

    def scatter_copy(i, send, recv, slot, rows, half, peer):
        return remote(
            send.at[slot, rows], recv.at[slot, rows],
            rs_send.at[i, half, slot], rs_recv.at[i, half, slot], dp, tensor ^ peer,
        )

    def scatter_first(i, send, recv, part):
        def far(k, carry):
            send[k] = part(k)
            scatter_copy(i, send, recv, k, late, 1, 4).start()

            @pl.when(k > 4)
            def _():
                scatter_copy(i, send, recv, k, early, 0, k - 4).start()

            return carry

        def near(k, carry):
            send[k] = part(k)
            scatter_copy(i, send, recv, k, early, 0, k).start()
            return carry

        lax.fori_loop(4, parts, far, 0)
        lax.fori_loop(1, 4, near, 0)
        send[0] = part(0)

    def scatter_second(i, send, recv):
        total = send[4, early].astype(f32)
        for k in (5, 6, 7):
            scatter_copy(i, send, recv, k, early, 0, k - 4).wait_recv()
            total = total + recv[k, early].astype(f32)
        send[4, early] = total.astype(bf16)
        scatter_copy(i, send, recv, 4, early, 0, 4).start()
        for k in (1, 2, 3):
            scatter_copy(i, send, recv, 4 + k, late, 1, 4).wait_recv()
            both_parts = send[k, late].astype(f32) + recv[4 + k, late].astype(f32)
            send[k, late] = both_parts.astype(bf16)
            scatter_copy(i, send, recv, k, late, 1, k).start()

    def scatter_rest(i, send, recv):
        rest = [scatter_copy(i, send, recv, k, early, 0, k) for k in (1, 2, 3)]
        rest.append(scatter_copy(i, send, recv, 4, late, 1, 4))
        rest.append(scatter_copy(i, send, recv, 4, early, 0, 4))
        rest += [scatter_copy(i, send, recv, k, late, 1, k) for k in (1, 2, 3)]
        return rest

    def layer_part(k):
        return jnp.dot(hidden[...], wd[:, at(k)], preferred_element_type=f32).astype(bf16)

    scatter_first(0, layer_send, layer_recv, layer_part)
    for copy in cot_second[0] + cot_second[1]:
        copy.wait_recv()

    mean_ref[...] = jnp.zeros_like(mean_ref)

    def backward(j, carry):
        here = pl.ds(pl.multiple_of(j * 128, 128), 128)
        hgrad = lax.dot_general(cotf[...], wd[here, :], NT, preferred_element_type=f32)
        ggug[:, pl.ds(pl.multiple_of(j * 256, 256), 128)] = (hgrad * dact[:, here]).astype(bf16)
        ggug[:, pl.ds(pl.multiple_of(j * 256 + 128, 128), 128)] = (
            hgrad * act[:, here]
        ).astype(bf16)
        mean_ref[...] += hgrad * both[:, here]
        return carry

    lax.fori_loop(0, pieces, backward, 0)
    mean = jnp.sum(mean_ref[...], axis=1, keepdims=True) * (1.0 / (parts * width))
    mean_ref[...] = jnp.broadcast_to(mean * scale_ref[:, :1], (cap, 128))
    scatter_second(0, layer_send, layer_recv)

    def grad_part(k):
        terms = lax.dot_general(
            ggug[:, : 2 * units], wgu[at(k), :], NT, preferred_element_type=f32
        )
        unit_part = tokf[:, at(k)].astype(f32) * mean_ref[:, :1]
        return (scale_ref[:, :1] * (terms * gain_ref[:, at(k)].astype(f32) - unit_part)).astype(
            bf16
        )

    scatter_first(1, grad_send, grad_recv, grad_part)

    def way_home(i, back, out, k):
        if k == 0:
            return pltpu.make_async_copy(back.at[0], out.at[:, :, 0], out_send.at[i, 0])
        return remote(
            back.at[k], out.at[:, :, k], out_send.at[i, k], out_recv.at[i, k],
            base + (own - k + GROUP) % GROUP, tensor,
        )

    def finish(i, full, send, recv, back, out):
        for copy in scatter_rest(i, send, recv):
            copy.wait_recv()
        result = full[:, at(0)].astype(f32) + send[0].astype(f32)
        for k in range(1, 5):
            result = result + recv[k].astype(f32)
        result = result.astype(bf16)
        for k in (4, 5, 3, 2, 6, 7, 1, 0):
            inside = lax.broadcasted_iota(i32, (seqs * seg, 1), 0)
            here = jnp.full((seqs * seg, 1), -1, i32)
            for s in range(seqs):
                pos = inside - s * seg
                n = k * seqs + s
                here = jnp.where((pos >= 0) & (pos < counts[n]), pos + starts[n], here)
            column = lax.broadcasted_iota(i32, (seqs * seg, cap), 1)
            spread = jnp.where(column == here, 1.0, 0.0).astype(bf16)
            rows = jnp.dot(spread, result, preferred_element_type=f32)
            back[k] = rows.reshape(seqs, rounds, TILE, width).astype(bf16)
            way_home(i, back, out, k).start()

    finish(0, tokf, layer_send, layer_recv, layer_back, layer_ref)
    scatter_second(1, grad_send, grad_recv)
    finish(1, cotf, grad_send, grad_recv, grad_back, grad_ref)

    for copy in cot_in[1:]:
        copy.wait_send()
    for copy in tok_first + tok_second[0] + tok_second[1] + cot_first + cot_second[0] + cot_second[1]:
        copy.wait_send()
    for i, (send, recv) in enumerate(((layer_send, layer_recv), (grad_send, grad_recv))):
        for copy in scatter_rest(i, send, recv):
            copy.wait_send()
        for k in (1, 2, 3):
            scatter_copy(i, send, recv, 4 + k, early, 0, k).wait_send()
            scatter_copy(i, send, recv, 4 + k, late, 1, 4).wait_send()
    for i, (back, out) in enumerate(((layer_back, layer_ref), (grad_back, grad_ref))):
        for k in range(GROUP):
            way_home(i, back, out, k).wait()


def layer(cap, number, info, tok, cotangent, gain, gate_weight, up_weight, down_weight, seqs):
    rows, width = tok.shape
    units, features = down_weight.shape
    parts = features // width
    rounds = rows // (seqs * GROUP * TILE)
    split = cap * 4 // 10 // 16 * 16
    tiled = (seqs, rounds, GROUP, TILE, width)
    slots = (GROUP, seqs, rounds, TILE, width)
    out = jax.ShapeDtypeStruct(tiled, bf16)
    anywhere = pl.BlockSpec(memory_space=pl.ANY)
    vmem = pl.BlockSpec(memory_space=pltpu.VMEM)
    peer_buffer = pltpu.VMEM((parts, cap, width), bf16)
    layer_out, input_grad = pl.pallas_call(
        functools.partial(layer_kernel, cap, split, seqs, rounds),
        out_shape=(out, out),
        in_specs=[pl.BlockSpec(memory_space=pltpu.SMEM), vmem, vmem] + [anywhere] * 4,
        out_specs=(anywhere, anywhere),
        scratch_shapes=[
            pltpu.VMEM((features, 2 * units), bf16),
            pltpu.VMEM((units, features), bf16),
            pltpu.VMEM(slots, bf16),
            pltpu.VMEM((cap, features), bf16),
            pltpu.VMEM((cap, features), bf16),
            pltpu.VMEM((cap, units), bf16),
            pltpu.VMEM((cap, units), f32),
            pltpu.VMEM((cap, units), f32),
            pltpu.VMEM((cap, units), f32),
            pltpu.VMEM((cap, max(features, 2 * units)), bf16),
            pltpu.VMEM((cap, 128), f32),
            pltpu.VMEM((cap, 128), f32),
            peer_buffer, peer_buffer, peer_buffer, peer_buffer,
            pltpu.VMEM(slots, bf16),
            pltpu.VMEM(slots, bf16),
            pltpu.SemaphoreType.DMA((2 * (units // 128) + 1,)),
            pltpu.SemaphoreType.DMA((GROUP,)),
            pltpu.SemaphoreType.DMA((GROUP,)),
            pltpu.SemaphoreType.DMA((2, 11)),
            pltpu.SemaphoreType.DMA((2, 11)),
            pltpu.SemaphoreType.DMA((2, 2, parts)),
            pltpu.SemaphoreType.DMA((2, 2, parts)),
            pltpu.SemaphoreType.DMA((2, GROUP)),
            pltpu.SemaphoreType.DMA((2, GROUP)),
        ],
        compiler_params=pltpu.CompilerParams(
            collective_id=number, has_side_effects=True, vmem_limit_bytes=62 << 20
        ),
        name=f"layer_{cap}",
    )(
        info, tok, gain.reshape(1, -1), cotangent.reshape(tiled),
        gate_weight, up_weight, down_weight,
    )
    return layer_out.reshape(rows, width), input_grad.reshape(rows, width)


def shards(tokens, gain, gate_weight, up_weight, down_weight, cotangent, lengths):
    tok, info, choice = exchange(tokens, lengths, lax.axis_size("dp"))

    def sized(number, cap):
        return lambda: layer(
            cap, number, info, tok, cotangent, gain, gate_weight, up_weight, down_weight,
            lengths.shape[0],
        )

    return lax.switch(choice, [sized(i + 1, cap) for i, cap in enumerate(CAPACITIES)])


def solution(mesh):
    placed = (
        P("dp", "tensor"),
        P(),
        P(None, "tensor"),
        P(None, "tensor"),
        P("tensor", None),
        P("dp", "tensor"),
        P("dp"),
    )
    return jax.shard_map(
        shards,
        mesh=mesh,
        in_specs=placed,
        out_specs=(P("dp", "tensor"), P("dp", "tensor")),
        check_vma=False,
    )
```

```python
import functools

import jax
import jax.numpy as jnp
from jax import lax
from jax.experimental import pallas as pl
from jax.experimental.pallas import tpu as pltpu
from jax.sharding import PartitionSpec as P

EPSILON = 1e-05
GROUP = 8
TILE = 8
CAPACITIES = (304, 336, 368, 416, 1024)
LARGE = 512
CHECK_AT = 3
MESH = pl.DeviceIdType.MESH
NT = (((1,), (1,)), ((), ()))
f32, bf16, i32 = jnp.float32, jnp.bfloat16, jnp.int32


def remote(src, dst, send_sem, recv_sem, dp, tensor):
    return pltpu.make_async_remote_copy(
        src_ref=src, dst_ref=dst, send_sem=send_sem, recv_sem=recv_sem,
        device_id=(dp, tensor), device_id_type=MESH,
    )


def signal(sem, dp, tensor):
    pl.semaphore_signal(sem, inc=1, device_id=(dp, tensor), device_id_type=MESH)


def tile_count(length, k):
    cycle = GROUP * TILE
    return length // cycle * TILE + jnp.clip(length % cycle - TILE * k, 0, TILE)


def exchange_kernel(
    planes, len_ref, tok_ref, tok_out, info_out, choice_ref,
    info, most, local_sem, send_sem, recv_sem, info_send, info_recv, most_send, most_recv,
):
    members = planes * GROUP
    dp = lax.axis_index("dp")
    tensor = lax.axis_index("tensor")
    plane = dp // GROUP
    base = plane * GROUP
    own = dp % GROUP
    seqs = len_ref.shape[0]
    barrier = pltpu.get_barrier_semaphore()

    def loop(low, high, step):
        def body(n, carry):
            step(n)
            return carry

        lax.fori_loop(low, high, body, 0)

    loop(1, GROUP, lambda k: signal(barrier, base + (own + k) % GROUP, tensor))
    loop(1, planes, lambda k: signal(barrier, (dp + k * GROUP) % members, tensor))
    local = pltpu.make_async_copy(tok_ref.at[:, :, 0], tok_out.at[0], local_sem.at[0])
    local.start()
    lane = lax.broadcasted_iota(i32, (1, 128), 1)
    phase = (lane + GROUP - own) % GROUP
    held = jnp.zeros((1, 128), i32)
    for s in range(seqs):
        held = held + tile_count(len_ref[s], phase)
    held = jnp.where(lane < GROUP, held, 0)
    for s in range(seqs):
        held = jnp.where(lane == GROUP + s, len_ref[s], held)
    info[...] = held
    info_out[own] = held
    pl.semaphore_wait(barrier, GROUP - 1 + planes - 1)

    def share(k):
        return remote(
            info, info_out.at[own], info_send.at[k], info_recv.at[k],
            base + (own + k) % GROUP, tensor,
        )

    def rows_to(k):
        return remote(
            tok_ref.at[:, :, k], tok_out.at[k], send_sem.at[k], recv_sem.at[k],
            base + (own + k) % GROUP, tensor,
        )

    def top(k):
        return remote(
            most.at[0], most.at[k], most_send.at[k], most_recv.at[k],
            (dp + k * GROUP) % members, tensor,
        )

    loop(1, GROUP, lambda k: share(k).start())
    loop(1, GROUP, lambda k: rows_to(k).start())
    loop(1, GROUP, lambda k: share(k).wait_recv())
    load = info_out[0]
    for h in range(1, GROUP):
        load = load + info_out[h]
    most[0] = load
    loop(1, planes, lambda k: top(k).start())
    loop(1, planes, lambda k: top(k).wait_recv())
    for k in range(1, planes):
        load = jnp.maximum(load, most[k])
    largest = jnp.max(jnp.where(lane < GROUP, load, 0))
    choice = jnp.int32(0)
    for cap in CAPACITIES[:-1]:
        choice = choice + (largest > cap).astype(i32)
    choice_ref[0] = choice
    loop(1, GROUP, lambda k: share(k).wait_send())
    loop(1, planes, lambda k: top(k).wait_send())
    local.wait()
    loop(1, GROUP, lambda k: rows_to(k).wait())


def exchange(tokens, lengths, members):
    seqs = lengths.shape[0]
    rows, width = tokens.shape
    rounds = rows // (seqs * GROUP * TILE)
    planes = members // GROUP
    slots = jax.ShapeDtypeStruct((GROUP, seqs, rounds, TILE, width), tokens.dtype)
    anywhere = pl.BlockSpec(memory_space=pl.ANY)
    smem = pl.BlockSpec(memory_space=pltpu.SMEM)
    tok, shared, choice = pl.pallas_call(
        functools.partial(exchange_kernel, planes),
        out_shape=(
            slots, jax.ShapeDtypeStruct((GROUP, 1, 128), i32), jax.ShapeDtypeStruct((1,), i32)
        ),
        in_specs=[smem, anywhere],
        out_specs=(anywhere, pl.BlockSpec(memory_space=pltpu.VMEM), smem),
        scratch_shapes=[
            pltpu.VMEM((1, 128), i32),
            pltpu.VMEM((planes, 1, 128), i32),
            pltpu.SemaphoreType.DMA((1,)),
            pltpu.SemaphoreType.DMA((GROUP,)),
            pltpu.SemaphoreType.DMA((GROUP,)),
            pltpu.SemaphoreType.DMA((GROUP,)),
            pltpu.SemaphoreType.DMA((GROUP,)),
            pltpu.SemaphoreType.DMA((planes,)),
            pltpu.SemaphoreType.DMA((planes,)),
        ],
        compiler_params=pltpu.CompilerParams(collective_id=0, has_side_effects=True),
        name="exchange",
    )(lengths, tokens.reshape(seqs, rounds, GROUP, TILE, width))
    return tok.reshape(rows, width), shared, choice[0]


def layer_kernel(
    cap, split, seqs, rounds,
    info_ref, tok_slots, gain_in, cot_ref, wg_ref, wu_ref, wd_ref,
    out_ref,
    wgu, wd, cot_slots, gain_ref, place_ref, acc, half, counts_ref, starts_ref,
    full, hidden, act, dact, both, ggug, scale_ref, mean_ref, send, recv, back,
    w_sem, in_send, in_recv, ag_send, ag_recv, rs_send, rs_recv, out_send, out_recv,
):
    dp = lax.axis_index("dp")
    tensor = lax.axis_index("tensor")
    base = dp // GROUP * GROUP
    own = dp % GROUP
    width = tok_slots.shape[1]
    parts = full.shape[2] // width
    units = wd_ref.shape[0]
    seg = rounds * TILE
    pieces = units // 128
    early, late = pl.ds(0, split), pl.ds(split, cap - split)

    def loop(low, high, step):
        def body(n, carry):
            step(n)
            return carry

        lax.fori_loop(low, high, body, 0)

    def chunk(c, size=width):
        return pl.ds(pl.multiple_of(c * size, size), size)

    def at(k):
        return chunk(tensor ^ k)

    def weight_copy(j, source, side):
        return pltpu.make_async_copy(
            source.at[:, chunk(j, 128)],
            wgu.at[:, pl.ds(pl.multiple_of(j * 256 + side * 128, 128), 128)],
            w_sem.at[2 * j + side],
        )

    down_copy = pltpu.make_async_copy(wd_ref, wd.at[pl.ds(0, units)], w_sem.at[2 * pieces])

    barrier = pltpu.get_barrier_semaphore()
    loop(1, 5, lambda k: signal(barrier, dp, tensor ^ k))
    loop(1, GROUP, lambda k: signal(barrier, base + (own + k) % GROUP, tensor))

    keep = pltpu.make_async_copy(cot_ref.at[:, :, 0], cot_slots.at[0], in_send.at[0])
    keep.start()

    def cot_in(k):
        return remote(
            cot_ref.at[:, :, k], cot_slots.at[k], in_send.at[k], in_recv.at[k],
            base + (own + k) % GROUP, tensor,
        )

    gain_ref[...] = gain_in[...].astype(f32).reshape(1, -1)
    spare = wd.shape[0] - units
    if spare:
        wd[pl.ds(units, spare), :] = jnp.zeros((spare, wd.shape[1]), bf16)
        hidden[:, pl.ds(units, spare)] = jnp.zeros((cap, spare), bf16)

    slot_rows = GROUP * seqs * seg
    lane = lax.broadcasted_iota(i32, (1, slot_rows), 1)
    place_ref[...] = jnp.full((1, slot_rows), -1, i32)

    def locate(m, total):
        k, s = m // seqs, m % seqs
        count = tile_count(info_ref[(own - k + GROUP) % GROUP, 0, GROUP + s], k)
        counts_ref[m] = count
        starts_ref[m] = total
        inside = lane - m * seg
        place_ref[...] = jnp.where(
            (inside >= 0) & (inside < count), inside + total, place_ref[...]
        )
        return total + count

    lax.fori_loop(0, GROUP * seqs, locate, jnp.int32(0))

    def accumulate(total, depth, term):
        if cap <= LARGE:
            total[...] = term(pl.ds(0, depth))
            return
        total[...] = jnp.zeros_like(total)

        def step(c):
            total[...] += term(chunk(c))

        loop(0, depth // width, step)

    def compact(i, slots):
        def term(c):
            row = lax.broadcasted_iota(i32, (cap, c.size), 0)
            picks = jnp.where(row == place_ref[:, c], 1.0, 0.0).astype(bf16)
            return jnp.dot(picks, slots[c, :], preferred_element_type=f32)

        accumulate(acc, slot_rows, term)
        full[i, :, at(0)] = acc[...].astype(bf16)

    def first_hop(i, k):
        return remote(
            full.at[i, :, at(0)], full.at[i, :, at(0)],
            ag_send.at[i, k], ag_recv.at[i, k], dp, tensor ^ k,
        )

    def to_y(i, k):
        return remote(
            full.at[i, early, at(4)], full.at[i, early, at(4)],
            ag_send.at[i, 4 + k], ag_recv.at[i, 4 + k], dp, tensor ^ k,
        )

    def to_z(i, k):
        return remote(
            full.at[i, late, at(k)], full.at[i, late, at(k)],
            ag_send.at[i, 7 + k], ag_recv.at[i, 7 + k], dp, tensor ^ 4,
        )

    def pass_from_z(i):
        first_hop(i, 4).wait_recv()
        loop(1, 4, lambda k: to_y(i, k).start())

    def pass_from_y(i):
        def step(k):
            first_hop(i, k).wait_recv()
            to_z(i, k).start()

        loop(1, 4, step)

    def arrive(i):
        def step(k):
            to_y(i, k).wait_recv()
            to_z(i, k).wait_recv()

        loop(1, 4, step)

    compact(0, tok_slots)
    pl.semaphore_wait(barrier, 4 + GROUP - 1)
    loop(0, 4, lambda n: first_hop(0, 4 - n).start())
    loop(1, GROUP, lambda k: cot_in(k).start())

    def fetch(j):
        weight_copy(j, wg_ref, 0).start()
        weight_copy(j, wu_ref, 1).start()

    loop(0, pieces, fetch)
    down_copy.start()
    pass_from_z(0)
    keep.wait()
    loop(1, GROUP, lambda k: cot_in(k).wait_recv())
    compact(1, cot_slots.reshape(slot_rows, width))
    pass_from_y(0)
    loop(0, 4, lambda n: first_hop(1, 4 - n).start())
    arrive(0)

    mean_ref[...] = jnp.zeros_like(mean_ref)

    def square(b):
        x = full[0, :, chunk(b, 128)].astype(f32)
        mean_ref[...] += x * x

    loop(0, parts * width // 128, square)
    total_sq = jnp.sum(mean_ref[...], axis=1, keepdims=True)
    scaler = lax.rsqrt(total_sq * (1.0 / (parts * width)) + EPSILON)
    scale_ref[...] = jnp.broadcast_to(scaler, (cap, 128))
    normed = ggug

    def norm(b):
        here = chunk(b, 128)
        x = full[0, :, here].astype(f32)
        normed[:, here] = (x * scale_ref[...] * gain_ref[:, here]).astype(bf16)

    loop(0, parts * width // 128, norm)

    def fetched(j):
        weight_copy(j, wg_ref, 0).wait()
        weight_copy(j, wu_ref, 1).wait()

    loop(0, pieces, fetched)
    down_copy.wait()
    pass_from_z(1)

    def forward(j):
        here = chunk(j, 128)
        accumulate(
            acc, parts * width,
            lambda c: jnp.dot(
                normed[:, c], wgu[c, chunk(j, 256)], preferred_element_type=f32
            ),
        )
        gate, up = acc[:, :128], acc[:, 128:]
        sigmoid = jax.nn.sigmoid(gate)
        silu = gate * sigmoid
        slope = up * sigmoid * (1.0 + gate * (1.0 - sigmoid))
        hidden[:, here] = (silu * up).astype(bf16)
        act[:, here] = silu
        dact[:, here] = slope
        both[:, here] = slope * gate + silu * up

        @pl.when(j == CHECK_AT)
        def _():
            pass_from_y(1)

    loop(0, pieces, forward)

    def early_copy(i, slot, peer):
        return remote(
            send.at[i, slot, early], recv.at[i, slot, early],
            rs_send.at[i, 0, slot], rs_recv.at[i, 0, slot], dp, tensor ^ peer,
        )

    def late_copy(i, slot, peer):
        return remote(
            send.at[i, slot, late], recv.at[i, slot, late],
            rs_send.at[i, 1, slot], rs_recv.at[i, 1, slot], dp, tensor ^ peer,
        )

    def scatter_first(i, part):
        def step(n):
            k = (n + 4) % parts
            part(k)

            @pl.when(k >= 4)
            def _():
                late_copy(i, k, 4).start()

            @pl.when((k > 0) & (k != 4))
            def _():
                early_copy(i, k, k % 4).start()

        loop(1, parts + 1, step)

    def scatter_second(i):
        acc[early, :] = send[i, 4, early].astype(f32)

        def across(k):
            early_copy(i, 4 + k, k).wait_recv()
            acc[early, :] += recv[i, 4 + k, early].astype(f32)

        loop(1, 4, across)
        send[i, 4, early] = acc[early, :].astype(bf16)
        early_copy(i, 4, 4).start()

        def along(k):
            late_copy(i, 4 + k, 4).wait_recv()
            pair = send[i, k, late].astype(f32) + recv[i, 4 + k, late].astype(f32)
            send[i, k, late] = pair.astype(bf16)
            late_copy(i, k, k).start()

        loop(1, 4, along)

    def layer_part(k):
        accumulate(
            acc, units if cap <= LARGE else hidden.shape[1],
            lambda c: jnp.dot(hidden[:, c], wd[c, at(k)], preferred_element_type=f32),
        )
        send[0, k] = acc[...].astype(bf16)

    scatter_first(0, layer_part)
    arrive(1)

    mean_ref[...] = jnp.zeros_like(mean_ref)

    def backward(j):
        here = chunk(j, 128)
        accumulate(
            half, parts * width,
            lambda c: lax.dot_general(
                full[1, :, c], wd[here, c], NT, preferred_element_type=f32
            ),
        )
        hgrad = half[...]
        ggug[:, pl.ds(pl.multiple_of(j * 256, 256), 128)] = (hgrad * dact[:, here]).astype(bf16)
        ggug[:, pl.ds(pl.multiple_of(j * 256 + 128, 128), 128)] = (
            hgrad * act[:, here]
        ).astype(bf16)
        mean_ref[...] += hgrad * both[:, here]

    loop(0, pieces, backward)
    mean = jnp.sum(mean_ref[...], axis=1, keepdims=True) * (1.0 / (parts * width))
    mean_ref[...] = jnp.broadcast_to(mean, (cap, 128)) * scale_ref[...]
    scatter_second(0)

    def grad_part(k):
        accumulate(
            acc, 2 * units,
            lambda c: lax.dot_general(
                ggug[:, c], wgu[at(k), c], NT, preferred_element_type=f32
            ),
        )
        unit_part = full[0, :, at(k)].astype(f32) * mean_ref[:, :1]
        send[1, k] = (scale_ref[:, :1] * (acc[...] * gain_ref[:, at(k)] - unit_part)).astype(bf16)

    scatter_first(1, grad_part)

    def stay(i):
        return pltpu.make_async_copy(back.at[i, 0], out_ref.at[i, :, :, 0], out_send.at[i, 0])

    def way_home(i, k):
        return remote(
            back.at[i, k], out_ref.at[i, :, :, k], out_send.at[i, k], out_recv.at[i, k],
            base + (own - k + GROUP) % GROUP, tensor,
        )

    def finish(i):
        @pl.when(i == 1)
        def _():
            scatter_second(1)

        acc[...] = full[i, :, at(0)].astype(f32) + send[i, 0].astype(f32)

        def add_early(k):
            early_copy(i, k, k).wait_recv()
            acc[early, :] += recv[i, k, early].astype(f32)

        loop(1, 5, add_early)

        def add_late(n):
            k = 5 - n
            late_copy(i, k, k).wait_recv()
            acc[late, :] += recv[i, k, late].astype(f32)

        loop(1, 5, add_late)
        hidden[:, :width] = acc[...].astype(bf16)

        def expand(n):
            k = (n + 3) % GROUP
            inside = lax.broadcasted_iota(i32, (seqs * seg, 1), 0)
            here = jnp.full((seqs * seg, 1), -1, i32)
            for s in range(seqs):
                pos = inside - s * seg
                m = k * seqs + s
                here = jnp.where((pos >= 0) & (pos < counts_ref[m]), pos + starts_ref[m], here)
            column = lax.broadcasted_iota(i32, (seqs * seg, cap), 1)
            spread = jnp.where(column == here, 1.0, 0.0).astype(bf16)
            rows = jnp.dot(spread, hidden[:, :width], preferred_element_type=f32)
            back[i, k] = rows.reshape(seqs, rounds, TILE, width).astype(bf16)

            @pl.when(k > 0)
            def _():
                way_home(i, k).start()

        loop(0, GROUP, expand)
        stay(i).start()

    loop(0, 2, finish)

    loop(1, GROUP, lambda k: cot_in(k).wait_send())

    def drain(i):
        loop(1, 5, lambda k: first_hop(i, k).wait_send())
        loop(1, 4, lambda k: to_y(i, k).wait_send())
        loop(1, 4, lambda k: to_z(i, k).wait_send())
        loop(1, parts, lambda k: early_copy(i, k, 1).wait_send())
        loop(1, parts, lambda k: late_copy(i, k, 1).wait_send())
        stay(i).wait()
        loop(1, GROUP, lambda k: way_home(i, k).wait())

    loop(0, 2, drain)


def layer(cap, number, info, tok, cotangent, gain, gate_weight, up_weight, down_weight, seqs):
    rows, width = tok.shape
    units, features = down_weight.shape
    padded = (units + 255) // 256 * 256
    parts = features // width
    rounds = rows // (seqs * GROUP * TILE)
    split = cap // 2 // 16 * 16
    tiled = (seqs, rounds, GROUP, TILE, width)
    slots = (GROUP, seqs, rounds, TILE, width)
    dma = pltpu.SemaphoreType.DMA
    anywhere = pl.BlockSpec(memory_space=pl.ANY)
    vmem = pl.BlockSpec(memory_space=pltpu.VMEM)
    return pl.pallas_call(
        functools.partial(layer_kernel, cap, split, seqs, rounds),
        out_shape=jax.ShapeDtypeStruct((2,) + tiled, bf16),
        in_specs=[pl.BlockSpec(memory_space=pltpu.SMEM), vmem, vmem] + [anywhere] * 4,
        out_specs=anywhere,
        scratch_shapes=[
            pltpu.VMEM((features, 2 * units), bf16),
            pltpu.VMEM((padded, features), bf16),
            pltpu.VMEM(slots, bf16),
            pltpu.VMEM((1, features), f32),
            pltpu.VMEM((1, rows), i32),
            pltpu.VMEM((cap, width), f32),
            pltpu.VMEM((cap, 128), f32),
            pltpu.SMEM((GROUP * seqs,), i32),
            pltpu.SMEM((GROUP * seqs,), i32),
            pltpu.VMEM((2, cap, features), bf16),
            pltpu.VMEM((cap, padded), bf16),
            pltpu.VMEM((cap, units), f32),
            pltpu.VMEM((cap, units), f32),
            pltpu.VMEM((cap, units), f32),
            pltpu.VMEM((cap, max(features, 2 * units)), bf16),
            pltpu.VMEM((cap, 128), f32),
            pltpu.VMEM((cap, 128), f32),
            pltpu.VMEM((2, parts, cap, width), bf16),
            pltpu.VMEM((2, parts, cap, width), bf16),
            pltpu.VMEM((2,) + slots, bf16),
            dma((2 * (units // 128) + 1,)),
            dma((GROUP,)),
            dma((GROUP,)),
            dma((2, 11)),
            dma((2, 11)),
            dma((2, 2, parts)),
            dma((2, 2, parts)),
            dma((2, GROUP)),
            dma((2, GROUP)),
        ],
        compiler_params=pltpu.CompilerParams(
            collective_id=number, has_side_effects=True, vmem_limit_bytes=62 << 20
        ),
        name=f"layer_{cap}",
    )(info, tok, gain, cotangent.reshape(tiled), gate_weight, up_weight, down_weight)


def shards(tokens, gain, gate_weight, up_weight, down_weight, cotangent, lengths):
    tok, info, choice = exchange(tokens, lengths, lax.axis_size("dp"))

    def sized(number, cap):
        return lambda: layer(
            cap, number, info, tok, cotangent, gain, gate_weight, up_weight, down_weight,
            lengths.shape[0],
        )

    out = lax.switch(choice, [sized(i + 1, cap) for i, cap in enumerate(CAPACITIES)])
    return out[0].reshape(tokens.shape), out[1].reshape(tokens.shape)


def solution(mesh):
    placed = (
        P("dp", "tensor"),
        P(),
        P(None, "tensor"),
        P(None, "tensor"),
        P("tensor", None),
        P("dp", "tensor"),
        P("dp"),
    )
    return jax.shard_map(
        shards,
        mesh=mesh,
        in_specs=placed,
        out_specs=(P("dp", "tensor"), P("dp", "tensor")),
        check_vma=False,
    )
```

```python
import functools

import jax
import jax.numpy as jnp
from jax import lax
from jax.experimental import pallas as pl
from jax.experimental.pallas import tpu as pltpu
from jax.sharding import PartitionSpec as P

EPSILON = 1e-05
GROUP = 8
TILE = 8
CAPACITIES = (304, 336, 368, 416, 1024)
LARGE = 512
CHECK_AT = 3
MESH = pl.DeviceIdType.MESH
NT = (((1,), (1,)), ((), ()))
f32, bf16, i32 = jnp.float32, jnp.bfloat16, jnp.int32


def remote(src, dst, send_sem, recv_sem, dp, tensor):
    return pltpu.make_async_remote_copy(
        src_ref=src, dst_ref=dst, send_sem=send_sem, recv_sem=recv_sem,
        device_id=(dp, tensor), device_id_type=MESH,
    )


def signal(sem, dp, tensor):
    pl.semaphore_signal(sem, inc=1, device_id=(dp, tensor), device_id_type=MESH)


def tile_count(length, k):
    cycle = GROUP * TILE
    return length // cycle * TILE + jnp.clip(length % cycle - TILE * k, 0, TILE)


def exchange_kernel(
    planes, len_ref, tok_ref, tok_out, info_out, choice_ref,
    info, most, local_sem, send_sem, recv_sem, info_send, info_recv, most_send, most_recv,
):
    members = planes * GROUP
    dp = lax.axis_index("dp")
    tensor = lax.axis_index("tensor")
    plane = dp // GROUP
    base = plane * GROUP
    own = dp % GROUP
    seqs = len_ref.shape[0]
    barrier = pltpu.get_barrier_semaphore()

    def loop(low, high, step):
        def body(n, carry):
            step(n)
            return carry

        lax.fori_loop(low, high, body, 0)

    loop(1, GROUP, lambda k: signal(barrier, base + (own + k) % GROUP, tensor))
    loop(1, planes, lambda k: signal(barrier, (dp + k * GROUP) % members, tensor))
    local = pltpu.make_async_copy(tok_ref.at[:, :, 0], tok_out.at[0], local_sem.at[0])
    local.start()
    lane = lax.broadcasted_iota(i32, (1, 128), 1)
    phase = (lane + GROUP - own) % GROUP
    held = jnp.zeros((1, 128), i32)
    for s in range(seqs):
        held = held + tile_count(len_ref[s], phase)
    held = jnp.where(lane < GROUP, held, 0)
    for s in range(seqs):
        held = jnp.where(lane == GROUP + s, len_ref[s], held)
    info[...] = held
    info_out[own] = held
    pl.semaphore_wait(barrier, GROUP - 1 + planes - 1)

    def share(k):
        return remote(
            info, info_out.at[own], info_send.at[k], info_recv.at[k],
            base + (own + k) % GROUP, tensor,
        )

    def rows_to(k):
        return remote(
            tok_ref.at[:, :, k], tok_out.at[k], send_sem.at[k], recv_sem.at[k],
            base + (own + k) % GROUP, tensor,
        )

    def top(k):
        return remote(
            most.at[0], most.at[k], most_send.at[k], most_recv.at[k],
            (dp + k * GROUP) % members, tensor,
        )

    loop(1, GROUP, lambda k: share(k).start())
    loop(1, GROUP, lambda k: rows_to(k).start())
    loop(1, GROUP, lambda k: share(k).wait_recv())
    load = info_out[0]
    for h in range(1, GROUP):
        load = load + info_out[h]
    most[0] = load
    loop(1, planes, lambda k: top(k).start())
    loop(1, planes, lambda k: top(k).wait_recv())
    for k in range(1, planes):
        load = jnp.maximum(load, most[k])
    largest = jnp.max(jnp.where(lane < GROUP, load, 0))
    choice = jnp.int32(0)
    for cap in CAPACITIES[:-1]:
        choice = choice + (largest > cap).astype(i32)
    choice_ref[0] = choice
    loop(1, GROUP, lambda k: share(k).wait_send())
    loop(1, planes, lambda k: top(k).wait_send())
    local.wait()
    loop(1, GROUP, lambda k: rows_to(k).wait())


def exchange(tokens, lengths, members):
    seqs = lengths.shape[0]
    rows, width = tokens.shape
    rounds = rows // (seqs * GROUP * TILE)
    planes = members // GROUP
    slots = jax.ShapeDtypeStruct((GROUP, seqs, rounds, TILE, width), tokens.dtype)
    anywhere = pl.BlockSpec(memory_space=pl.ANY)
    smem = pl.BlockSpec(memory_space=pltpu.SMEM)
    tok, shared, choice = pl.pallas_call(
        functools.partial(exchange_kernel, planes),
        out_shape=(
            slots, jax.ShapeDtypeStruct((GROUP, 1, 128), i32), jax.ShapeDtypeStruct((1,), i32)
        ),
        in_specs=[smem, anywhere],
        out_specs=(anywhere, pl.BlockSpec(memory_space=pltpu.VMEM), smem),
        scratch_shapes=[
            pltpu.VMEM((1, 128), i32),
            pltpu.VMEM((planes, 1, 128), i32),
            pltpu.SemaphoreType.DMA((1,)),
            pltpu.SemaphoreType.DMA((GROUP,)),
            pltpu.SemaphoreType.DMA((GROUP,)),
            pltpu.SemaphoreType.DMA((GROUP,)),
            pltpu.SemaphoreType.DMA((GROUP,)),
            pltpu.SemaphoreType.DMA((planes,)),
            pltpu.SemaphoreType.DMA((planes,)),
        ],
        compiler_params=pltpu.CompilerParams(collective_id=0, has_side_effects=True),
        name="exchange",
    )(lengths, tokens.reshape(seqs, rounds, GROUP, TILE, width))
    return tok.reshape(rows, width), shared, choice[0]


def layer_kernel(
    cap, split, cut, seqs, rounds,
    info_ref, tok_slots, gain_in, cot_ref, wg_ref, wu_ref, wd_ref,
    out_ref,
    wgu, wd, cot_slots, gain_ref, place_ref, acc, half, counts_ref, starts_ref,
    full, hidden, act, dact, both, ggug, scale_ref, mean_ref, send, recv, back,
    w_sem, in_send, in_recv, ag_send, ag_recv, rs_send, rs_recv, out_send, out_recv,
):
    dp = lax.axis_index("dp")
    tensor = lax.axis_index("tensor")
    base = dp // GROUP * GROUP
    own = dp % GROUP
    width = tok_slots.shape[1]
    parts = full.shape[2] // width
    units = wd_ref.shape[0]
    seg = rounds * TILE
    pieces = units // 128
    early, late = pl.ds(0, split), pl.ds(split, cap - split)

    def loop(low, high, step):
        def body(n, carry):
            step(n)
            return carry

        lax.fori_loop(low, high, body, 0)

    def chunk(c, size=width):
        return pl.ds(pl.multiple_of(c * size, size), size)

    def at(k):
        return chunk(tensor ^ k)

    def weight_copy(j, source, side):
        return pltpu.make_async_copy(
            source.at[:, chunk(j, 128)],
            wgu.at[:, pl.ds(pl.multiple_of(j * 256 + side * 128, 128), 128)],
            w_sem.at[2 * j + side],
        )

    down_copy = pltpu.make_async_copy(wd_ref, wd.at[pl.ds(0, units)], w_sem.at[2 * pieces])

    barrier = pltpu.get_barrier_semaphore()
    loop(1, 5, lambda k: signal(barrier, dp, tensor ^ k))
    loop(1, GROUP, lambda k: signal(barrier, base + (own + k) % GROUP, tensor))

    keep = pltpu.make_async_copy(cot_ref.at[:, :, 0], cot_slots.at[0], in_send.at[0])
    keep.start()

    def cot_in(k):
        return remote(
            cot_ref.at[:, :, k], cot_slots.at[k], in_send.at[k], in_recv.at[k],
            base + (own + k) % GROUP, tensor,
        )

    gain_ref[...] = gain_in[...].astype(f32).reshape(1, -1)
    spare = wd.shape[0] - units
    if spare:
        wd[pl.ds(units, spare), :] = jnp.zeros((spare, wd.shape[1]), bf16)
        hidden[:, pl.ds(units, spare)] = jnp.zeros((cap, spare), bf16)

    slot_rows = GROUP * seqs * seg
    lane = lax.broadcasted_iota(i32, (1, slot_rows), 1)
    place_ref[...] = jnp.full((1, slot_rows), -1, i32)

    def locate(m, total):
        k, s = m // seqs, m % seqs
        count = tile_count(info_ref[(own - k + GROUP) % GROUP, 0, GROUP + s], k)
        counts_ref[m] = count
        starts_ref[m] = total
        inside = lane - m * seg
        place_ref[...] = jnp.where(
            (inside >= 0) & (inside < count), inside + total, place_ref[...]
        )
        return total + count

    lax.fori_loop(0, GROUP * seqs, locate, jnp.int32(0))

    def accumulate(total, depth, term):
        if cap <= LARGE:
            total[...] = term(pl.ds(0, depth))
            return
        total[...] = jnp.zeros_like(total)

        def step(c):
            total[...] += term(chunk(c))

        loop(0, depth // width, step)

    def compact(i, slots):
        def term(c):
            row = lax.broadcasted_iota(i32, (cap, c.size), 0)
            picks = jnp.where(row == place_ref[:, c], 1.0, 0.0).astype(bf16)
            return jnp.dot(picks, slots[c, :], preferred_element_type=f32)

        accumulate(acc, slot_rows, term)
        full[i, :, at(0)] = acc[...].astype(bf16)

    def first_hop(i, k):
        return remote(
            full.at[i, :, at(0)], full.at[i, :, at(0)],
            ag_send.at[i, k], ag_recv.at[i, k], dp, tensor ^ k,
        )

    def ring(i, k):
        rows = early if k == 1 else late
        return remote(
            full.at[i, rows, at(k)], full.at[i, rows, at(k)],
            ag_send.at[i, 10 + k], ag_recv.at[i, 10 + k], dp, tensor ^ (4 - k),
        )

    def to_y(i, k):
        return remote(
            full.at[i, early, at(4)], full.at[i, early, at(4)],
            ag_send.at[i, 4 + k], ag_recv.at[i, 4 + k], dp, tensor ^ k,
        )

    def to_z(i, k):
        return remote(
            full.at[i, late, at(k)], full.at[i, late, at(k)],
            ag_send.at[i, 7 + k], ag_recv.at[i, 7 + k], dp, tensor ^ 4,
        )

    def set_out(i):
        for k in (4, 1, 3):
            first_hop(i, k).start()

    def pass_on(i):
        for k in (1, 3):
            first_hop(i, k).wait_recv()
            ring(i, k).start()
            to_z(i, k).start()
        first_hop(i, 4).wait_recv()
        loop(1, 4, lambda k: to_y(i, k).start())

    def pass_last(i):
        ring(i, 3).wait_recv()
        to_z(i, 2).start()

    def arrive(i):
        ring(i, 1).wait_recv()

        def step(k):
            to_y(i, k).wait_recv()
            to_z(i, k).wait_recv()

        loop(1, 4, step)

    compact(0, tok_slots)
    pl.semaphore_wait(barrier, 4 + GROUP - 1)
    set_out(0)
    loop(1, GROUP, lambda k: cot_in(k).start())

    def fetch(j):
        weight_copy(j, wg_ref, 0).start()
        weight_copy(j, wu_ref, 1).start()

    loop(0, pieces, fetch)
    down_copy.start()
    pass_on(0)
    keep.wait()
    loop(1, GROUP, lambda k: cot_in(k).wait_recv())
    compact(1, cot_slots.reshape(slot_rows, width))
    pass_last(0)
    set_out(1)
    arrive(0)

    mean_ref[...] = jnp.zeros_like(mean_ref)

    def square(b):
        x = full[0, :, chunk(b, 128)].astype(f32)
        mean_ref[...] += x * x

    loop(0, parts * width // 128, square)
    total_sq = jnp.sum(mean_ref[...], axis=1, keepdims=True)
    scaler = lax.rsqrt(total_sq * (1.0 / (parts * width)) + EPSILON)
    scale_ref[...] = jnp.broadcast_to(scaler, (cap, 128))
    normed = ggug

    def norm(b):
        here = chunk(b, 128)
        x = full[0, :, here].astype(f32)
        normed[:, here] = (x * scale_ref[...] * gain_ref[:, here]).astype(bf16)

    loop(0, parts * width // 128, norm)

    def fetched(j):
        weight_copy(j, wg_ref, 0).wait()
        weight_copy(j, wu_ref, 1).wait()

    loop(0, pieces, fetched)
    down_copy.wait()
    pass_on(1)

    def forward(j):
        here = chunk(j, 128)
        accumulate(
            acc, parts * width,
            lambda c: jnp.dot(
                normed[:, c], wgu[c, chunk(j, 256)], preferred_element_type=f32
            ),
        )
        gate, up = acc[:, :128], acc[:, 128:]
        sigmoid = jax.nn.sigmoid(gate)
        silu = gate * sigmoid
        slope = up * sigmoid * (1.0 + gate * (1.0 - sigmoid))
        hidden[:, here] = (silu * up).astype(bf16)
        act[:, here] = silu
        dact[:, here] = slope
        both[:, here] = slope * gate + silu * up

        @pl.when(j == CHECK_AT)
        def _():
            pass_last(1)

    loop(0, pieces, forward)

    upper, lower = pl.ds(0, cut), pl.ds(cut, cap - cut)

    def upper_copy(i, slot, peer):
        return remote(
            send.at[i, slot, upper], recv.at[i, slot, upper],
            rs_send.at[i, 0, slot], rs_recv.at[i, 0, slot], dp, tensor ^ peer,
        )

    def lower_copy(i, slot, peer):
        return remote(
            send.at[i, slot, lower], recv.at[i, slot, lower],
            rs_send.at[i, 1, slot], rs_recv.at[i, 1, slot], dp, tensor ^ peer,
        )

    def scatter_first(i, part):
        def step(n):
            k = (n + 4) % parts
            part(k)

            @pl.when(k >= 4)
            def _():
                lower_copy(i, k, 4).start()

            @pl.when((k > 0) & (k != 4))
            def _():
                upper_copy(i, k, k % 4).start()

        loop(1, parts + 1, step)

    def scatter_second(i):
        acc[upper, :] = send[i, 4, upper].astype(f32)

        def across(k):
            upper_copy(i, 4 + k, k).wait_recv()
            acc[upper, :] += recv[i, 4 + k, upper].astype(f32)

        loop(1, 4, across)
        send[i, 4, upper] = acc[upper, :].astype(bf16)
        upper_copy(i, 4, 4).start()

        def along(k):
            lower_copy(i, 4 + k, 4).wait_recv()
            pair = send[i, k, lower].astype(f32) + recv[i, 4 + k, lower].astype(f32)
            send[i, k, lower] = pair.astype(bf16)
            lower_copy(i, k, k).start()

        loop(1, 4, along)

    def layer_part(k):
        accumulate(
            acc, units if cap <= LARGE else hidden.shape[1],
            lambda c: jnp.dot(hidden[:, c], wd[c, at(k)], preferred_element_type=f32),
        )
        send[0, k] = acc[...].astype(bf16)

    scatter_first(0, layer_part)
    arrive(1)

    mean_ref[...] = jnp.zeros_like(mean_ref)

    def backward(j):
        here = chunk(j, 128)
        accumulate(
            half, parts * width,
            lambda c: lax.dot_general(
                full[1, :, c], wd[here, c], NT, preferred_element_type=f32
            ),
        )
        hgrad = half[...]
        ggug[:, pl.ds(pl.multiple_of(j * 256, 256), 128)] = (hgrad * dact[:, here]).astype(bf16)
        ggug[:, pl.ds(pl.multiple_of(j * 256 + 128, 128), 128)] = (
            hgrad * act[:, here]
        ).astype(bf16)
        mean_ref[...] += hgrad * both[:, here]

    loop(0, pieces, backward)
    mean = jnp.sum(mean_ref[...], axis=1, keepdims=True) * (1.0 / (parts * width))
    mean_ref[...] = jnp.broadcast_to(mean, (cap, 128)) * scale_ref[...]
    scatter_second(0)

    def grad_part(k):
        accumulate(
            acc, 2 * units,
            lambda c: lax.dot_general(
                ggug[:, c], wgu[at(k), c], NT, preferred_element_type=f32
            ),
        )
        unit_part = full[0, :, at(k)].astype(f32) * mean_ref[:, :1]
        send[1, k] = (scale_ref[:, :1] * (acc[...] * gain_ref[:, at(k)] - unit_part)).astype(bf16)

    scatter_first(1, grad_part)

    def stay(i):
        return pltpu.make_async_copy(back.at[i, 0], out_ref.at[i, :, :, 0], out_send.at[i, 0])

    def way_home(i, k):
        return remote(
            back.at[i, k], out_ref.at[i, :, :, k], out_send.at[i, k], out_recv.at[i, k],
            base + (own - k + GROUP) % GROUP, tensor,
        )

    def finish(i):
        @pl.when(i == 1)
        def _():
            scatter_second(1)

        acc[...] = full[i, :, at(0)].astype(f32) + send[i, 0].astype(f32)

        def add_upper(k):
            upper_copy(i, k, k).wait_recv()
            acc[upper, :] += recv[i, k, upper].astype(f32)

        loop(1, 5, add_upper)

        def add_lower(n):
            k = 5 - n
            lower_copy(i, k, k).wait_recv()
            acc[lower, :] += recv[i, k, lower].astype(f32)

        loop(1, 5, add_lower)
        hidden[:, :width] = acc[...].astype(bf16)

        def expand(n):
            k = (n + 3) % GROUP
            inside = lax.broadcasted_iota(i32, (seqs * seg, 1), 0)
            here = jnp.full((seqs * seg, 1), -1, i32)
            for s in range(seqs):
                pos = inside - s * seg
                m = k * seqs + s
                here = jnp.where((pos >= 0) & (pos < counts_ref[m]), pos + starts_ref[m], here)
            column = lax.broadcasted_iota(i32, (seqs * seg, cap), 1)
            spread = jnp.where(column == here, 1.0, 0.0).astype(bf16)
            rows = jnp.dot(spread, hidden[:, :width], preferred_element_type=f32)
            back[i, k] = rows.reshape(seqs, rounds, TILE, width).astype(bf16)

            @pl.when(k > 0)
            def _():
                way_home(i, k).start()

        loop(0, GROUP, expand)
        stay(i).start()

    loop(0, 2, finish)

    loop(1, GROUP, lambda k: cot_in(k).wait_send())

    def drain(i):
        for k in (1, 3, 4):
            first_hop(i, k).wait_send()
        for k in (1, 3):
            ring(i, k).wait_send()
        loop(1, 4, lambda k: to_y(i, k).wait_send())
        loop(1, 4, lambda k: to_z(i, k).wait_send())
        loop(1, parts, lambda k: upper_copy(i, k, 1).wait_send())
        loop(1, parts, lambda k: lower_copy(i, k, 1).wait_send())
        stay(i).wait()
        loop(1, GROUP, lambda k: way_home(i, k).wait())

    loop(0, 2, drain)


def layer(cap, number, info, tok, cotangent, gain, gate_weight, up_weight, down_weight, seqs):
    rows, width = tok.shape
    units, features = down_weight.shape
    padded = (units + 255) // 256 * 256
    parts = features // width
    rounds = rows // (seqs * GROUP * TILE)
    split = cap // 2 // 16 * 16
    cut = cap * 5 // 10 // 16 * 16
    tiled = (seqs, rounds, GROUP, TILE, width)
    slots = (GROUP, seqs, rounds, TILE, width)
    dma = pltpu.SemaphoreType.DMA
    anywhere = pl.BlockSpec(memory_space=pl.ANY)
    vmem = pl.BlockSpec(memory_space=pltpu.VMEM)
    return pl.pallas_call(
        functools.partial(layer_kernel, cap, split, cut, seqs, rounds),
        out_shape=jax.ShapeDtypeStruct((2,) + tiled, bf16),
        in_specs=[pl.BlockSpec(memory_space=pltpu.SMEM), vmem, vmem] + [anywhere] * 4,
        out_specs=anywhere,
        scratch_shapes=[
            pltpu.VMEM((features, 2 * units), bf16),
            pltpu.VMEM((padded, features), bf16),
            pltpu.VMEM(slots, bf16),
            pltpu.VMEM((1, features), f32),
            pltpu.VMEM((1, rows), i32),
            pltpu.VMEM((cap, width), f32),
            pltpu.VMEM((cap, 128), f32),
            pltpu.SMEM((GROUP * seqs,), i32),
            pltpu.SMEM((GROUP * seqs,), i32),
            pltpu.VMEM((2, cap, features), bf16),
            pltpu.VMEM((cap, padded), bf16),
            pltpu.VMEM((cap, units), f32),
            pltpu.VMEM((cap, units), f32),
            pltpu.VMEM((cap, units), f32),
            pltpu.VMEM((cap, max(features, 2 * units)), bf16),
            pltpu.VMEM((cap, 128), f32),
            pltpu.VMEM((cap, 128), f32),
            pltpu.VMEM((2, parts, cap, width), bf16),
            pltpu.VMEM((2, parts, cap, width), bf16),
            pltpu.VMEM((2,) + slots, bf16),
            dma((2 * (units // 128) + 1,)),
            dma((GROUP,)),
            dma((GROUP,)),
            dma((2, 14)),
            dma((2, 14)),
            dma((2, 2, parts)),
            dma((2, 2, parts)),
            dma((2, GROUP)),
            dma((2, GROUP)),
        ],
        compiler_params=pltpu.CompilerParams(
            collective_id=number, has_side_effects=True, vmem_limit_bytes=62 << 20
        ),
        name=f"layer_{cap}",
    )(info, tok, gain, cotangent.reshape(tiled), gate_weight, up_weight, down_weight)


def shards(tokens, gain, gate_weight, up_weight, down_weight, cotangent, lengths):
    tok, info, choice = exchange(tokens, lengths, lax.axis_size("dp"))

    def sized(number, cap):
        return lambda: layer(
            cap, number, info, tok, cotangent, gain, gate_weight, up_weight, down_weight,
            lengths.shape[0],
        )

    out = lax.switch(choice, [sized(i + 1, cap) for i, cap in enumerate(CAPACITIES)])
    return out[0].reshape(tokens.shape), out[1].reshape(tokens.shape)


def solution(mesh):
    placed = (
        P("dp", "tensor"),
        P(),
        P(None, "tensor"),
        P(None, "tensor"),
        P("tensor", None),
        P("dp", "tensor"),
        P("dp"),
    )
    return jax.shard_map(
        shards,
        mesh=mesh,
        in_specs=placed,
        out_specs=(P("dp", "tensor"), P("dp", "tensor")),
        check_vma=False,
    )
```

```python
import functools

import jax
import jax.numpy as jnp
from jax import lax
from jax.experimental import pallas as pl
from jax.experimental.pallas import tpu as pltpu
from jax.sharding import PartitionSpec as P

EPSILON = 1e-05
GROUP = 8
TILE = 8
CAPACITIES = (320, 336, 352, 368, 400, 480, 1024)
LARGE = 512
CHECK_AT = 3
MESH = pl.DeviceIdType.MESH
NT = (((1,), (1,)), ((), ()))
f32, bf16, i32 = jnp.float32, jnp.bfloat16, jnp.int32


def remote(src, dst, send_sem, recv_sem, dp, tensor):
    return pltpu.make_async_remote_copy(
        src_ref=src, dst_ref=dst, send_sem=send_sem, recv_sem=recv_sem,
        device_id=(dp, tensor), device_id_type=MESH,
    )


def signal(sem, dp, tensor):
    pl.semaphore_signal(sem, inc=1, device_id=(dp, tensor), device_id_type=MESH)


def tile_count(length, k):
    cycle = GROUP * TILE
    return length // cycle * TILE + jnp.clip(length % cycle - TILE * k, 0, TILE)


def exchange_kernel(
    planes, len_ref, tok_ref, tok_out, info_out, choice_ref,
    info, most, local_sem, send_sem, recv_sem, info_send, info_recv, most_send, most_recv,
):
    members = planes * GROUP
    dp = lax.axis_index("dp")
    tensor = lax.axis_index("tensor")
    plane = dp // GROUP
    base = plane * GROUP
    own = dp % GROUP
    seqs = len_ref.shape[0]
    barrier = pltpu.get_barrier_semaphore()

    def loop(low, high, step):
        def body(n, carry):
            step(n)
            return carry

        lax.fori_loop(low, high, body, 0)

    loop(1, GROUP, lambda k: signal(barrier, base + (own + k) % GROUP, tensor))
    loop(1, planes, lambda k: signal(barrier, (dp + k * GROUP) % members, tensor))
    local = pltpu.make_async_copy(tok_ref.at[:, :, 0], tok_out.at[0], local_sem.at[0])
    local.start()
    lane = lax.broadcasted_iota(i32, (1, 128), 1)
    phase = (lane + GROUP - own) % GROUP
    held = jnp.zeros((1, 128), i32)
    for s in range(seqs):
        held = held + tile_count(len_ref[s], phase)
    held = jnp.where(lane < GROUP, held, 0)
    for s in range(seqs):
        held = jnp.where(lane == GROUP + s, len_ref[s], held)
    info[...] = held
    info_out[own] = held
    pl.semaphore_wait(barrier, GROUP - 1 + planes - 1)

    def share(k):
        return remote(
            info, info_out.at[own], info_send.at[k], info_recv.at[k],
            base + (own + k) % GROUP, tensor,
        )

    def rows_to(k):
        return remote(
            tok_ref.at[:, :, k], tok_out.at[k], send_sem.at[k], recv_sem.at[k],
            base + (own + k) % GROUP, tensor,
        )

    def top(k):
        return remote(
            most.at[0], most.at[k], most_send.at[k], most_recv.at[k],
            (dp + k * GROUP) % members, tensor,
        )

    loop(1, GROUP, lambda k: share(k).start())
    loop(1, GROUP, lambda k: rows_to(k).start())
    loop(1, GROUP, lambda k: share(k).wait_recv())
    load = info_out[0]
    for h in range(1, GROUP):
        load = load + info_out[h]
    most[0] = load
    loop(1, planes, lambda k: top(k).start())
    loop(1, planes, lambda k: top(k).wait_recv())
    for k in range(1, planes):
        load = jnp.maximum(load, most[k])
    largest = jnp.max(jnp.where(lane < GROUP, load, 0))
    choice = jnp.int32(0)
    for cap in CAPACITIES[:-1]:
        choice = choice + (largest > cap).astype(i32)
    choice_ref[0] = choice
    loop(1, GROUP, lambda k: share(k).wait_send())
    loop(1, planes, lambda k: top(k).wait_send())
    local.wait()
    loop(1, GROUP, lambda k: rows_to(k).wait())


def exchange(tokens, lengths, members):
    seqs = lengths.shape[0]
    rows, width = tokens.shape
    rounds = rows // (seqs * GROUP * TILE)
    planes = members // GROUP
    slots = jax.ShapeDtypeStruct((GROUP, seqs, rounds, TILE, width), tokens.dtype)
    anywhere = pl.BlockSpec(memory_space=pl.ANY)
    smem = pl.BlockSpec(memory_space=pltpu.SMEM)
    tok, shared, choice = pl.pallas_call(
        functools.partial(exchange_kernel, planes),
        out_shape=(
            slots, jax.ShapeDtypeStruct((GROUP, 1, 128), i32), jax.ShapeDtypeStruct((1,), i32)
        ),
        in_specs=[smem, anywhere],
        out_specs=(anywhere, pl.BlockSpec(memory_space=pltpu.VMEM), smem),
        scratch_shapes=[
            pltpu.VMEM((1, 128), i32),
            pltpu.VMEM((planes, 1, 128), i32),
            pltpu.SemaphoreType.DMA((1,)),
            pltpu.SemaphoreType.DMA((GROUP,)),
            pltpu.SemaphoreType.DMA((GROUP,)),
            pltpu.SemaphoreType.DMA((GROUP,)),
            pltpu.SemaphoreType.DMA((GROUP,)),
            pltpu.SemaphoreType.DMA((planes,)),
            pltpu.SemaphoreType.DMA((planes,)),
        ],
        compiler_params=pltpu.CompilerParams(collective_id=0, has_side_effects=True),
        name="exchange",
    )(lengths, tokens.reshape(seqs, rounds, GROUP, TILE, width))
    return tok.reshape(rows, width), shared, choice[0]


def layer_kernel(
    cap, split, cut, seqs, rounds,
    info_ref, tok_slots, gain_in, cot_ref, wg_ref, wu_ref, wd_ref,
    out_ref,
    wgu, wd, cot_slots, gain_ref, place_ref, acc, half, counts_ref, starts_ref,
    full, hidden, act, dact, both, ggug, scale_ref, mean_ref, send, recv, back,
    w_sem, in_send, in_recv, ag_send, ag_recv, rs_send, rs_recv, out_send, out_recv,
):
    dp = lax.axis_index("dp")
    tensor = lax.axis_index("tensor")
    base = dp // GROUP * GROUP
    own = dp % GROUP
    width = tok_slots.shape[1]
    parts = full.shape[2] // width
    units = wd_ref.shape[0]
    seg = rounds * TILE
    pieces = units // 128
    early, late = pl.ds(0, split), pl.ds(split, cap - split)

    def loop(low, high, step):
        def body(n, carry):
            step(n)
            return carry

        lax.fori_loop(low, high, body, 0)

    def chunk(c, size=width):
        return pl.ds(pl.multiple_of(c * size, size), size)

    def at(k):
        return chunk(tensor ^ k)

    def weight_copy(j, source, side):
        return pltpu.make_async_copy(
            source.at[:, chunk(j, 128)],
            wgu.at[:, pl.ds(pl.multiple_of(j * 256 + side * 128, 128), 128)],
            w_sem.at[2 * j + side],
        )

    down_copy = pltpu.make_async_copy(wd_ref, wd.at[pl.ds(0, units)], w_sem.at[2 * pieces])

    barrier = pltpu.get_barrier_semaphore()
    loop(1, 5, lambda k: signal(barrier, dp, tensor ^ k))
    loop(1, GROUP, lambda k: signal(barrier, base + (own + k) % GROUP, tensor))

    keep = pltpu.make_async_copy(cot_ref.at[:, :, 0], cot_slots.at[0], in_send.at[0])
    keep.start()

    def cot_in(k):
        return remote(
            cot_ref.at[:, :, k], cot_slots.at[k], in_send.at[k], in_recv.at[k],
            base + (own + k) % GROUP, tensor,
        )

    gain_ref[...] = gain_in[...].astype(f32).reshape(1, -1)
    spare = wd.shape[0] - units
    if spare:
        wd[pl.ds(units, spare), :] = jnp.zeros((spare, wd.shape[1]), bf16)
        hidden[:, pl.ds(units, spare)] = jnp.zeros((cap, spare), bf16)

    slot_rows = GROUP * seqs * seg
    lane = lax.broadcasted_iota(i32, (1, slot_rows), 1)
    place_ref[...] = jnp.full((1, slot_rows), -1, i32)

    def locate(m, total):
        k, s = m // seqs, m % seqs
        count = tile_count(info_ref[(own - k + GROUP) % GROUP, 0, GROUP + s], k)
        counts_ref[m] = count
        starts_ref[m] = total
        inside = lane - m * seg
        place_ref[...] = jnp.where(
            (inside >= 0) & (inside < count), inside + total, place_ref[...]
        )
        return total + count

    lax.fori_loop(0, GROUP * seqs, locate, jnp.int32(0))

    def accumulate(total, depth, term):
        if cap <= LARGE:
            total[...] = term(pl.ds(0, depth))
            return
        total[...] = jnp.zeros_like(total)

        def step(c):
            total[...] += term(chunk(c))

        loop(0, depth // width, step)

    def compact(i, slots):
        def term(c):
            row = lax.broadcasted_iota(i32, (cap, c.size), 0)
            picks = jnp.where(row == place_ref[:, c], 1.0, 0.0).astype(bf16)
            return jnp.dot(picks, slots[c, :], preferred_element_type=f32)

        accumulate(acc, slot_rows, term)
        full[i, :, at(0)] = acc[...].astype(bf16)

    def first_hop(i, k):
        return remote(
            full.at[i, :, at(0)], full.at[i, :, at(0)],
            ag_send.at[i, k], ag_recv.at[i, k], dp, tensor ^ k,
        )

    def ring(i, k):
        rows = early if k == 1 else late
        return remote(
            full.at[i, rows, at(k)], full.at[i, rows, at(k)],
            ag_send.at[i, 10 + k], ag_recv.at[i, 10 + k], dp, tensor ^ (4 - k),
        )

    def to_y(i, k):
        return remote(
            full.at[i, early, at(4)], full.at[i, early, at(4)],
            ag_send.at[i, 4 + k], ag_recv.at[i, 4 + k], dp, tensor ^ k,
        )

    def to_z(i, k):
        return remote(
            full.at[i, late, at(k)], full.at[i, late, at(k)],
            ag_send.at[i, 7 + k], ag_recv.at[i, 7 + k], dp, tensor ^ 4,
        )

    def set_out(i):
        for k in (4, 1, 3):
            first_hop(i, k).start()

    def pass_on(i):
        for k in (1, 3):
            first_hop(i, k).wait_recv()
            ring(i, k).start()
            to_z(i, k).start()
        first_hop(i, 4).wait_recv()
        loop(1, 4, lambda k: to_y(i, k).start())

    def pass_last(i):
        ring(i, 3).wait_recv()
        to_z(i, 2).start()

    def arrive(i):
        ring(i, 1).wait_recv()

        def step(k):
            to_y(i, k).wait_recv()
            to_z(i, k).wait_recv()

        loop(1, 4, step)

    compact(0, tok_slots)
    pl.semaphore_wait(barrier, 4 + GROUP - 1)
    set_out(0)
    loop(1, GROUP, lambda k: cot_in(k).start())

    def fetch(j):
        weight_copy(j, wg_ref, 0).start()
        weight_copy(j, wu_ref, 1).start()

    loop(0, pieces, fetch)
    down_copy.start()
    pass_on(0)
    keep.wait()
    loop(1, GROUP, lambda k: cot_in(k).wait_recv())
    compact(1, cot_slots.reshape(slot_rows, width))
    pass_last(0)
    set_out(1)
    arrive(0)

    mean_ref[...] = jnp.zeros_like(mean_ref)

    def square(b):
        x = full[0, :, chunk(b, 128)].astype(f32)
        mean_ref[...] += x * x

    loop(0, parts * width // 128, square)
    total_sq = jnp.sum(mean_ref[...], axis=1, keepdims=True)
    scaler = lax.rsqrt(total_sq * (1.0 / (parts * width)) + EPSILON)
    scale_ref[...] = jnp.broadcast_to(scaler, (cap, 128))
    normed = ggug

    def norm(b):
        here = chunk(b, 128)
        x = full[0, :, here].astype(f32)
        normed[:, here] = (x * scale_ref[...] * gain_ref[:, here]).astype(bf16)

    loop(0, parts * width // 128, norm)

    def fetched(j):
        weight_copy(j, wg_ref, 0).wait()
        weight_copy(j, wu_ref, 1).wait()

    loop(0, pieces, fetched)
    down_copy.wait()
    pass_on(1)

    def forward(j):
        here = chunk(j, 128)
        accumulate(
            acc, parts * width,
            lambda c: jnp.dot(
                normed[:, c], wgu[c, chunk(j, 256)], preferred_element_type=f32
            ),
        )
        gate, up = acc[:, :128], acc[:, 128:]
        sigmoid = jax.nn.sigmoid(gate)
        silu = gate * sigmoid
        slope = up * sigmoid * (1.0 + gate * (1.0 - sigmoid))
        hidden[:, here] = (silu * up).astype(bf16)
        act[:, here] = silu
        dact[:, here] = slope
        both[:, here] = slope * gate + silu * up

        @pl.when(j == CHECK_AT)
        def _():
            pass_last(1)

    loop(0, pieces, forward)

    upper, lower = pl.ds(0, cut), pl.ds(cut, cap - cut)

    def upper_copy(i, slot, peer):
        return remote(
            send.at[i, slot, upper], recv.at[i, slot, upper],
            rs_send.at[i, 0, slot], rs_recv.at[i, 0, slot], dp, tensor ^ peer,
        )

    def lower_copy(i, slot, peer):
        return remote(
            send.at[i, slot, lower], recv.at[i, slot, lower],
            rs_send.at[i, 1, slot], rs_recv.at[i, 1, slot], dp, tensor ^ peer,
        )

    def scatter_first(i, part):
        def step(n):
            k = (n + 4) % parts
            part(k)

            @pl.when(k >= 4)
            def _():
                lower_copy(i, k, 4).start()

            @pl.when((k > 0) & (k != 4))
            def _():
                upper_copy(i, k, k % 4).start()

        loop(1, parts + 1, step)

    def scatter_second(i):
        acc[upper, :] = send[i, 4, upper].astype(f32)

        def across(k):
            upper_copy(i, 4 + k, k).wait_recv()
            acc[upper, :] += recv[i, 4 + k, upper].astype(f32)

        loop(1, 4, across)
        send[i, 4, upper] = acc[upper, :].astype(bf16)
        upper_copy(i, 4, 4).start()

        def along(k):
            lower_copy(i, 4 + k, 4).wait_recv()
            pair = send[i, k, lower].astype(f32) + recv[i, 4 + k, lower].astype(f32)
            send[i, k, lower] = pair.astype(bf16)
            lower_copy(i, k, k).start()

        loop(1, 4, along)

    def layer_part(k):
        accumulate(
            acc, units if cap <= LARGE else hidden.shape[1],
            lambda c: jnp.dot(hidden[:, c], wd[c, at(k)], preferred_element_type=f32),
        )
        send[0, k] = acc[...].astype(bf16)

    scatter_first(0, layer_part)
    arrive(1)

    mean_ref[...] = jnp.zeros_like(mean_ref)

    def backward(j):
        here = chunk(j, 128)
        accumulate(
            half, parts * width,
            lambda c: lax.dot_general(
                full[1, :, c], wd[here, c], NT, preferred_element_type=f32
            ),
        )
        hgrad = half[...]
        ggug[:, pl.ds(pl.multiple_of(j * 256, 256), 128)] = (hgrad * dact[:, here]).astype(bf16)
        ggug[:, pl.ds(pl.multiple_of(j * 256 + 128, 128), 128)] = (
            hgrad * act[:, here]
        ).astype(bf16)
        mean_ref[...] += hgrad * both[:, here]

    loop(0, pieces, backward)
    mean = jnp.sum(mean_ref[...], axis=1, keepdims=True) * (1.0 / (parts * width))
    mean_ref[...] = jnp.broadcast_to(mean, (cap, 128)) * scale_ref[...]
    scatter_second(0)

    def grad_part(k):
        accumulate(
            acc, 2 * units,
            lambda c: lax.dot_general(
                ggug[:, c], wgu[at(k), c], NT, preferred_element_type=f32
            ),
        )
        unit_part = full[0, :, at(k)].astype(f32) * mean_ref[:, :1]
        send[1, k] = (scale_ref[:, :1] * (acc[...] * gain_ref[:, at(k)] - unit_part)).astype(bf16)

    scatter_first(1, grad_part)

    def stay(i):
        return pltpu.make_async_copy(back.at[i, 0], out_ref.at[i, :, :, 0], out_send.at[i, 0])

    def way_home(i, k):
        return remote(
            back.at[i, k], out_ref.at[i, :, :, k], out_send.at[i, k], out_recv.at[i, k],
            base + (own - k + GROUP) % GROUP, tensor,
        )

    def finish(i):
        @pl.when(i == 1)
        def _():
            scatter_second(1)

        acc[...] = full[i, :, at(0)].astype(f32) + send[i, 0].astype(f32)

        def add_upper(k):
            upper_copy(i, k, k).wait_recv()
            acc[upper, :] += recv[i, k, upper].astype(f32)

        loop(1, 5, add_upper)

        def add_lower(n):
            k = 5 - n
            lower_copy(i, k, k).wait_recv()
            acc[lower, :] += recv[i, k, lower].astype(f32)

        loop(1, 5, add_lower)
        hidden[:, :width] = acc[...].astype(bf16)

        def expand(n):
            k = (n + 3) % GROUP
            inside = lax.broadcasted_iota(i32, (seqs * seg, 1), 0)
            here = jnp.full((seqs * seg, 1), -1, i32)
            for s in range(seqs):
                pos = inside - s * seg
                m = k * seqs + s
                here = jnp.where((pos >= 0) & (pos < counts_ref[m]), pos + starts_ref[m], here)
            column = lax.broadcasted_iota(i32, (seqs * seg, cap), 1)
            spread = jnp.where(column == here, 1.0, 0.0).astype(bf16)
            rows = jnp.dot(spread, hidden[:, :width], preferred_element_type=f32)
            back[i, k] = rows.reshape(seqs, rounds, TILE, width).astype(bf16)

            @pl.when(k > 0)
            def _():
                way_home(i, k).start()

        loop(0, GROUP, expand)
        stay(i).start()

    loop(0, 2, finish)

    loop(1, GROUP, lambda k: cot_in(k).wait_send())

    def drain(i):
        for k in (1, 3, 4):
            first_hop(i, k).wait_send()
        for k in (1, 3):
            ring(i, k).wait_send()
        loop(1, 4, lambda k: to_y(i, k).wait_send())
        loop(1, 4, lambda k: to_z(i, k).wait_send())
        loop(1, parts, lambda k: upper_copy(i, k, 1).wait_send())
        loop(1, parts, lambda k: lower_copy(i, k, 1).wait_send())
        stay(i).wait()
        loop(1, GROUP, lambda k: way_home(i, k).wait())

    loop(0, 2, drain)


def layer(cap, number, info, tok, cotangent, gain, gate_weight, up_weight, down_weight, seqs):
    rows, width = tok.shape
    units, features = down_weight.shape
    padded = (units + 255) // 256 * 256
    parts = features // width
    rounds = rows // (seqs * GROUP * TILE)
    split = cap // 2 // 16 * 16
    cut = cap * 5 // 10 // 16 * 16
    tiled = (seqs, rounds, GROUP, TILE, width)
    slots = (GROUP, seqs, rounds, TILE, width)
    dma = pltpu.SemaphoreType.DMA
    anywhere = pl.BlockSpec(memory_space=pl.ANY)
    vmem = pl.BlockSpec(memory_space=pltpu.VMEM)
    return pl.pallas_call(
        functools.partial(layer_kernel, cap, split, cut, seqs, rounds),
        out_shape=jax.ShapeDtypeStruct((2,) + tiled, bf16),
        in_specs=[pl.BlockSpec(memory_space=pltpu.SMEM), vmem, vmem] + [anywhere] * 4,
        out_specs=anywhere,
        scratch_shapes=[
            pltpu.VMEM((features, 2 * units), bf16),
            pltpu.VMEM((padded, features), bf16),
            pltpu.VMEM(slots, bf16),
            pltpu.VMEM((1, features), f32),
            pltpu.VMEM((1, rows), i32),
            pltpu.VMEM((cap, width), f32),
            pltpu.VMEM((cap, 128), f32),
            pltpu.SMEM((GROUP * seqs,), i32),
            pltpu.SMEM((GROUP * seqs,), i32),
            pltpu.VMEM((2, cap, features), bf16),
            pltpu.VMEM((cap, padded), bf16),
            pltpu.VMEM((cap, units), f32),
            pltpu.VMEM((cap, units), f32),
            pltpu.VMEM((cap, units), f32),
            pltpu.VMEM((cap, max(features, 2 * units)), bf16),
            pltpu.VMEM((cap, 128), f32),
            pltpu.VMEM((cap, 128), f32),
            pltpu.VMEM((2, parts, cap, width), bf16),
            pltpu.VMEM((2, parts, cap, width), bf16),
            pltpu.VMEM((2,) + slots, bf16),
            dma((2 * (units // 128) + 1,)),
            dma((GROUP,)),
            dma((GROUP,)),
            dma((2, 14)),
            dma((2, 14)),
            dma((2, 2, parts)),
            dma((2, 2, parts)),
            dma((2, GROUP)),
            dma((2, GROUP)),
        ],
        compiler_params=pltpu.CompilerParams(
            collective_id=number, has_side_effects=True, vmem_limit_bytes=62 << 20
        ),
        name=f"layer_{cap}",
    )(info, tok, gain, cotangent.reshape(tiled), gate_weight, up_weight, down_weight)


def shards(tokens, gain, gate_weight, up_weight, down_weight, cotangent, lengths):
    tok, info, choice = exchange(tokens, lengths, lax.axis_size("dp"))

    def sized(number, cap):
        return lambda: layer(
            cap, number, info, tok, cotangent, gain, gate_weight, up_weight, down_weight,
            lengths.shape[0],
        )

    out = lax.switch(choice, [sized(i + 1, cap) for i, cap in enumerate(CAPACITIES)])
    return out[0].reshape(tokens.shape), out[1].reshape(tokens.shape)


def solution(mesh):
    placed = (
        P("dp", "tensor"),
        P(),
        P(None, "tensor"),
        P(None, "tensor"),
        P("tensor", None),
        P("dp", "tensor"),
        P("dp"),
    )
    return jax.shard_map(
        shards,
        mesh=mesh,
        in_specs=placed,
        out_specs=(P("dp", "tensor"), P("dp", "tensor")),
        check_vma=False,
    )
```

```python
import functools

import jax
import jax.numpy as jnp
from jax import lax
from jax.experimental import pallas as pl
from jax.experimental.pallas import tpu as pltpu
from jax.sharding import PartitionSpec as P

EPSILON = 1e-05
GROUP = 8
TILE = 8
CAPACITIES = (320, 336, 352, 368, 400, 480, 1024)
LARGE = 512
CHECK_AT = 3
MESH = pl.DeviceIdType.MESH
NT = (((1,), (1,)), ((), ()))
f32, bf16, i32 = jnp.float32, jnp.bfloat16, jnp.int32


def remote(src, dst, send_sem, recv_sem, dp, tensor):
    return pltpu.make_async_remote_copy(
        src_ref=src, dst_ref=dst, send_sem=send_sem, recv_sem=recv_sem,
        device_id=(dp, tensor), device_id_type=MESH,
    )


def signal(sem, dp, tensor):
    pl.semaphore_signal(sem, inc=1, device_id=(dp, tensor), device_id_type=MESH)


def tile_count(length, k):
    cycle = GROUP * TILE
    return length // cycle * TILE + jnp.clip(length % cycle - TILE * k, 0, TILE)


def exchange_kernel(
    planes, len_ref, tok_ref, tok_out, info_out, choice_ref,
    info, most, local_sem, send_sem, recv_sem, info_send, info_recv, most_send, most_recv,
):
    members = planes * GROUP
    dp = lax.axis_index("dp")
    tensor = lax.axis_index("tensor")
    plane = dp // GROUP
    base = plane * GROUP
    own = dp % GROUP
    seqs = len_ref.shape[0]
    barrier = pltpu.get_barrier_semaphore()

    def loop(low, high, step):
        def body(n, carry):
            step(n)
            return carry

        lax.fori_loop(low, high, body, 0)

    loop(1, GROUP, lambda k: signal(barrier, base + (own + k) % GROUP, tensor))
    loop(1, planes, lambda k: signal(barrier, (dp + k * GROUP) % members, tensor))
    local = pltpu.make_async_copy(tok_ref.at[:, :, 0], tok_out.at[0], local_sem.at[0])
    local.start()
    lane = lax.broadcasted_iota(i32, (1, 128), 1)
    phase = (lane + GROUP - own) % GROUP
    held = jnp.zeros((1, 128), i32)
    for s in range(seqs):
        held = held + tile_count(len_ref[s], phase)
    held = jnp.where(lane < GROUP, held, 0)
    for s in range(seqs):
        held = jnp.where(lane == GROUP + s, len_ref[s], held)
    info[...] = held
    info_out[own] = held
    pl.semaphore_wait(barrier, GROUP - 1 + planes - 1)

    def share(k):
        return remote(
            info, info_out.at[own], info_send.at[k], info_recv.at[k],
            base + (own + k) % GROUP, tensor,
        )

    def rows_to(k):
        return remote(
            tok_ref.at[:, :, k], tok_out.at[k], send_sem.at[k], recv_sem.at[k],
            base + (own + k) % GROUP, tensor,
        )

    def top(k):
        return remote(
            most.at[0], most.at[k], most_send.at[k], most_recv.at[k],
            (dp + k * GROUP) % members, tensor,
        )

    loop(1, GROUP, lambda k: share(k).start())
    loop(1, GROUP, lambda k: rows_to(k).start())
    loop(1, GROUP, lambda k: share(k).wait_recv())
    load = info_out[0]
    for h in range(1, GROUP):
        load = load + info_out[h]
    most[0] = load
    loop(1, planes, lambda k: top(k).start())
    loop(1, planes, lambda k: top(k).wait_recv())
    for k in range(1, planes):
        load = jnp.maximum(load, most[k])
    largest = jnp.max(jnp.where(lane < GROUP, load, 0))
    choice = jnp.int32(0)
    for cap in CAPACITIES[:-1]:
        choice = choice + (largest > cap).astype(i32)
    choice_ref[0] = choice
    loop(1, GROUP, lambda k: share(k).wait_send())
    loop(1, planes, lambda k: top(k).wait_send())
    local.wait()
    loop(1, GROUP, lambda k: rows_to(k).wait())


def exchange(tokens, lengths, members):
    seqs = lengths.shape[0]
    rows, width = tokens.shape
    rounds = rows // (seqs * GROUP * TILE)
    planes = members // GROUP
    slots = jax.ShapeDtypeStruct((GROUP, seqs, rounds, TILE, width), tokens.dtype)
    anywhere = pl.BlockSpec(memory_space=pl.ANY)
    smem = pl.BlockSpec(memory_space=pltpu.SMEM)
    tok, shared, choice = pl.pallas_call(
        functools.partial(exchange_kernel, planes),
        out_shape=(
            slots, jax.ShapeDtypeStruct((GROUP, 1, 128), i32), jax.ShapeDtypeStruct((1,), i32)
        ),
        in_specs=[smem, anywhere],
        out_specs=(anywhere, pl.BlockSpec(memory_space=pltpu.VMEM), smem),
        scratch_shapes=[
            pltpu.VMEM((1, 128), i32),
            pltpu.VMEM((planes, 1, 128), i32),
            pltpu.SemaphoreType.DMA((1,)),
            pltpu.SemaphoreType.DMA((GROUP,)),
            pltpu.SemaphoreType.DMA((GROUP,)),
            pltpu.SemaphoreType.DMA((GROUP,)),
            pltpu.SemaphoreType.DMA((GROUP,)),
            pltpu.SemaphoreType.DMA((planes,)),
            pltpu.SemaphoreType.DMA((planes,)),
        ],
        compiler_params=pltpu.CompilerParams(collective_id=0, has_side_effects=True),
        name="exchange",
    )(lengths, tokens.reshape(seqs, rounds, GROUP, TILE, width))
    return tok.reshape(rows, width), shared, choice[0]


def layer_kernel(
    cap, split, cut, seqs, rounds,
    info_ref, tok_slots, gain_in, cot_ref, wg_ref, wu_ref, wd_ref,
    out_ref,
    wgu, wd, cot_slots, gain_ref, place_ref, acc, half, counts_ref, starts_ref,
    full, hidden, act, dact, both, ggug, scale_ref, mean_ref, send, recv, back,
    w_sem, in_send, in_recv, ag_send, ag_recv, rs_send, rs_recv, out_send, out_recv,
):
    dp = lax.axis_index("dp")
    tensor = lax.axis_index("tensor")
    base = dp // GROUP * GROUP
    own = dp % GROUP
    width = tok_slots.shape[1]
    parts = full.shape[2] // width
    units = wd_ref.shape[0]
    seg = rounds * TILE
    pieces = units // 128
    early, late = pl.ds(0, split), pl.ds(split, cap - split)

    def loop(low, high, step):
        def body(n, carry):
            step(n)
            return carry

        lax.fori_loop(low, high, body, 0)

    def chunk(c, size=width):
        return pl.ds(pl.multiple_of(c * size, size), size)

    def at(k):
        return chunk(tensor ^ k)

    def weight_copy(j, source, side):
        return pltpu.make_async_copy(
            source.at[:, chunk(j, 128)],
            wgu.at[:, pl.ds(pl.multiple_of(j * 256 + side * 128, 128), 128)],
            w_sem.at[2 * j + side],
        )

    down_copy = pltpu.make_async_copy(wd_ref, wd.at[pl.ds(0, units)], w_sem.at[2 * pieces])

    barrier = pltpu.get_barrier_semaphore()
    loop(1, 5, lambda k: signal(barrier, dp, tensor ^ k))
    loop(1, GROUP, lambda k: signal(barrier, base + (own + k) % GROUP, tensor))

    keep = pltpu.make_async_copy(cot_ref.at[:, :, 0], cot_slots.at[0], in_send.at[0])
    keep.start()

    def cot_in(k):
        return remote(
            cot_ref.at[:, :, k], cot_slots.at[k], in_send.at[k], in_recv.at[k],
            base + (own + k) % GROUP, tensor,
        )

    gain_ref[...] = gain_in[...].astype(f32).reshape(1, -1)
    spare = wd.shape[0] - units
    if spare:
        wd[pl.ds(units, spare), :] = jnp.zeros((spare, wd.shape[1]), bf16)
        hidden[:, pl.ds(units, spare)] = jnp.zeros((cap, spare), bf16)

    slot_rows = GROUP * seqs * seg
    lane = lax.broadcasted_iota(i32, (1, slot_rows), 1)
    place_ref[...] = jnp.full((1, slot_rows), -1, i32)

    def locate(m, total):
        k, s = m // seqs, m % seqs
        count = tile_count(info_ref[(own - k + GROUP) % GROUP, 0, GROUP + s], k)
        counts_ref[m] = count
        starts_ref[m] = total
        inside = lane - m * seg
        place_ref[...] = jnp.where(
            (inside >= 0) & (inside < count), inside + total, place_ref[...]
        )
        return total + count

    lax.fori_loop(0, GROUP * seqs, locate, jnp.int32(0))

    def accumulate(total, depth, term):
        if cap <= LARGE:
            total[...] = term(pl.ds(0, depth))
            return
        total[...] = jnp.zeros_like(total)

        def step(c):
            total[...] += term(chunk(c))

        loop(0, depth // width, step)

    def compact(i, slots):
        def term(c):
            row = lax.broadcasted_iota(i32, (cap, c.size), 0)
            picks = jnp.where(row == place_ref[:, c], 1.0, 0.0).astype(bf16)
            return jnp.dot(picks, slots[c, :], preferred_element_type=f32)

        accumulate(acc, slot_rows, term)
        full[i, :, at(0)] = acc[...].astype(bf16)

    def first_hop(i, k):
        return remote(
            full.at[i, :, at(0)], full.at[i, :, at(0)],
            ag_send.at[i, k], ag_recv.at[i, k], dp, tensor ^ k,
        )

    def ring(i, k):
        rows = early if k == 1 else late
        return remote(
            full.at[i, rows, at(k)], full.at[i, rows, at(k)],
            ag_send.at[i, 10 + k], ag_recv.at[i, 10 + k], dp, tensor ^ (4 - k),
        )

    def to_y(i, k):
        return remote(
            full.at[i, early, at(4)], full.at[i, early, at(4)],
            ag_send.at[i, 4 + k], ag_recv.at[i, 4 + k], dp, tensor ^ k,
        )

    def to_z(i, k):
        return remote(
            full.at[i, late, at(k)], full.at[i, late, at(k)],
            ag_send.at[i, 7 + k], ag_recv.at[i, 7 + k], dp, tensor ^ 4,
        )

    def set_out(i):
        for k in (4, 1, 3):
            first_hop(i, k).start()

    def pass_on(i):
        for k in (1, 3):
            first_hop(i, k).wait_recv()
            ring(i, k).start()
            to_z(i, k).start()
        first_hop(i, 4).wait_recv()
        loop(1, 4, lambda k: to_y(i, k).start())

    def pass_last(i):
        ring(i, 3).wait_recv()
        to_z(i, 2).start()

    def arrive(i):
        ring(i, 1).wait_recv()

        def step(k):
            to_y(i, k).wait_recv()
            to_z(i, k).wait_recv()

        loop(1, 4, step)

    compact(0, tok_slots)
    pl.semaphore_wait(barrier, 4 + GROUP - 1)
    set_out(0)
    loop(1, GROUP, lambda k: cot_in(k).start())

    def fetch(j):
        weight_copy(j, wg_ref, 0).start()
        weight_copy(j, wu_ref, 1).start()

    loop(0, pieces, fetch)
    down_copy.start()
    pass_on(0)
    keep.wait()
    loop(1, GROUP, lambda k: cot_in(k).wait_recv())
    compact(1, cot_slots.reshape(slot_rows, width))
    pass_last(0)
    set_out(1)
    arrive(0)

    mean_ref[...] = jnp.zeros_like(mean_ref)

    def square(b):
        x = full[0, :, chunk(b, 128)].astype(f32)
        mean_ref[...] += x * x

    loop(0, parts * width // 128, square)
    total_sq = jnp.sum(mean_ref[...], axis=1, keepdims=True)
    scaler = lax.rsqrt(total_sq * (1.0 / (parts * width)) + EPSILON)
    scale_ref[...] = jnp.broadcast_to(scaler, (cap, 128))
    normed = ggug

    def norm(b):
        here = chunk(b, 128)
        x = full[0, :, here].astype(f32)
        normed[:, here] = (x * scale_ref[...] * gain_ref[:, here]).astype(bf16)

    loop(0, parts * width // 128, norm)

    def fetched(j):
        weight_copy(j, wg_ref, 0).wait()
        weight_copy(j, wu_ref, 1).wait()

    loop(0, pieces, fetched)
    down_copy.wait()
    pass_on(1)

    def forward(j):
        here = chunk(j, 128)
        accumulate(
            acc, parts * width,
            lambda c: jnp.dot(
                normed[:, c], wgu[c, chunk(j, 256)], preferred_element_type=f32
            ),
        )
        gate, up = acc[:, :128], acc[:, 128:]
        sigmoid = jax.nn.sigmoid(gate)
        silu = gate * sigmoid
        slope = up * sigmoid * (1.0 + gate * (1.0 - sigmoid))
        hidden[:, here] = (silu * up).astype(bf16)
        act[:, here] = silu
        dact[:, here] = slope
        both[:, here] = slope * gate + silu * up

        @pl.when(j == CHECK_AT)
        def _():
            pass_last(1)

    loop(0, pieces, forward)

    upper, lower = pl.ds(0, cut), pl.ds(cut, cap - cut)

    def upper_copy(i, slot, peer):
        return remote(
            send.at[i, slot, upper], recv.at[i, slot, upper],
            rs_send.at[i, 0, slot], rs_recv.at[i, 0, slot], dp, tensor ^ peer,
        )

    def lower_copy(i, slot, peer):
        return remote(
            send.at[i, slot, lower], recv.at[i, slot, lower],
            rs_send.at[i, 1, slot], rs_recv.at[i, 1, slot], dp, tensor ^ peer,
        )

    def scatter_first(i, part):
        def step(n):
            k = jnp.where(n < 4, n + 4, jnp.where(n < 7, n - 3, 32 - 4 * n))
            part(k)

            @pl.when(k >= 4)
            def _():
                lower_copy(i, k, 4).start()

            @pl.when((k > 0) & (k != 4))
            def _():
                upper_copy(i, k, k % 4).start()

        loop(1, parts + 1, step)

    def scatter_second(i):
        acc[upper, :] = send[i, 4, upper].astype(f32)

        def across(k):
            upper_copy(i, 4 + k, k).wait_recv()
            acc[upper, :] += recv[i, 4 + k, upper].astype(f32)

        loop(1, 4, across)
        send[i, 4, upper] = acc[upper, :].astype(bf16)
        upper_copy(i, 4, 4).start()

        def along(k):
            lower_copy(i, 4 + k, 4).wait_recv()
            pair = send[i, k, lower].astype(f32) + recv[i, 4 + k, lower].astype(f32)
            send[i, k, lower] = pair.astype(bf16)
            lower_copy(i, k, k).start()

        loop(1, 4, along)

    def layer_part(k):
        accumulate(
            acc, units if cap <= LARGE else hidden.shape[1],
            lambda c: jnp.dot(hidden[:, c], wd[c, at(k)], preferred_element_type=f32),
        )
        send[0, k] = acc[...].astype(bf16)

    scatter_first(0, layer_part)
    arrive(1)

    mean_ref[...] = jnp.zeros_like(mean_ref)

    def backward(j):
        here = chunk(j, 128)
        accumulate(
            half, parts * width,
            lambda c: lax.dot_general(
                full[1, :, c], wd[here, c], NT, preferred_element_type=f32
            ),
        )
        hgrad = half[...]
        ggug[:, pl.ds(pl.multiple_of(j * 256, 256), 128)] = (hgrad * dact[:, here]).astype(bf16)
        ggug[:, pl.ds(pl.multiple_of(j * 256 + 128, 128), 128)] = (
            hgrad * act[:, here]
        ).astype(bf16)
        mean_ref[...] += hgrad * both[:, here]

    loop(0, pieces, backward)
    mean = jnp.sum(mean_ref[...], axis=1, keepdims=True) * (1.0 / (parts * width))
    mean_ref[...] = jnp.broadcast_to(mean, (cap, 128)) * scale_ref[...]
    scatter_second(0)

    def grad_part(k):
        accumulate(
            acc, 2 * units,
            lambda c: lax.dot_general(
                ggug[:, c], wgu[at(k), c], NT, preferred_element_type=f32
            ),
        )
        unit_part = full[0, :, at(k)].astype(f32) * mean_ref[:, :1]
        send[1, k] = (scale_ref[:, :1] * (acc[...] * gain_ref[:, at(k)] - unit_part)).astype(bf16)

    scatter_first(1, grad_part)

    def stay(i):
        return pltpu.make_async_copy(back.at[i, 0], out_ref.at[i, :, :, 0], out_send.at[i, 0])

    def way_home(i, k):
        return remote(
            back.at[i, k], out_ref.at[i, :, :, k], out_send.at[i, k], out_recv.at[i, k],
            base + (own - k + GROUP) % GROUP, tensor,
        )

    def finish(i):
        @pl.when(i == 1)
        def _():
            scatter_second(1)

        acc[...] = full[i, :, at(0)].astype(f32) + send[i, 0].astype(f32)

        def add_upper(k):
            upper_copy(i, k, k).wait_recv()
            acc[upper, :] += recv[i, k, upper].astype(f32)

        loop(1, 5, add_upper)

        def add_lower(n):
            k = 5 - n
            lower_copy(i, k, k).wait_recv()
            acc[lower, :] += recv[i, k, lower].astype(f32)

        loop(1, 5, add_lower)
        hidden[:, :width] = acc[...].astype(bf16)

        def expand(n):
            k = (n + 3) % GROUP
            inside = lax.broadcasted_iota(i32, (seqs * seg, 1), 0)
            here = jnp.full((seqs * seg, 1), -1, i32)
            for s in range(seqs):
                pos = inside - s * seg
                m = k * seqs + s
                here = jnp.where((pos >= 0) & (pos < counts_ref[m]), pos + starts_ref[m], here)
            column = lax.broadcasted_iota(i32, (seqs * seg, cap), 1)
            spread = jnp.where(column == here, 1.0, 0.0).astype(bf16)
            rows = jnp.dot(spread, hidden[:, :width], preferred_element_type=f32)
            back[i, k] = rows.reshape(seqs, rounds, TILE, width).astype(bf16)

            @pl.when(k > 0)
            def _():
                way_home(i, k).start()

        loop(0, GROUP, expand)
        stay(i).start()

    loop(0, 2, finish)

    loop(1, GROUP, lambda k: cot_in(k).wait_send())

    def drain(i):
        for k in (1, 3, 4):
            first_hop(i, k).wait_send()
        for k in (1, 3):
            ring(i, k).wait_send()
        loop(1, 4, lambda k: to_y(i, k).wait_send())
        loop(1, 4, lambda k: to_z(i, k).wait_send())
        loop(1, parts, lambda k: upper_copy(i, k, 1).wait_send())
        loop(1, parts, lambda k: lower_copy(i, k, 1).wait_send())
        stay(i).wait()
        loop(1, GROUP, lambda k: way_home(i, k).wait())

    loop(0, 2, drain)


def layer(cap, number, info, tok, cotangent, gain, gate_weight, up_weight, down_weight, seqs):
    rows, width = tok.shape
    units, features = down_weight.shape
    padded = (units + 255) // 256 * 256
    parts = features // width
    rounds = rows // (seqs * GROUP * TILE)
    split = cap // 2 // 16 * 16
    cut = cap * 5 // 10 // 16 * 16
    tiled = (seqs, rounds, GROUP, TILE, width)
    slots = (GROUP, seqs, rounds, TILE, width)
    dma = pltpu.SemaphoreType.DMA
    anywhere = pl.BlockSpec(memory_space=pl.ANY)
    vmem = pl.BlockSpec(memory_space=pltpu.VMEM)
    return pl.pallas_call(
        functools.partial(layer_kernel, cap, split, cut, seqs, rounds),
        out_shape=jax.ShapeDtypeStruct((2,) + tiled, bf16),
        in_specs=[pl.BlockSpec(memory_space=pltpu.SMEM), vmem, vmem] + [anywhere] * 4,
        out_specs=anywhere,
        scratch_shapes=[
            pltpu.VMEM((features, 2 * units), bf16),
            pltpu.VMEM((padded, features), bf16),
            pltpu.VMEM(slots, bf16),
            pltpu.VMEM((1, features), f32),
            pltpu.VMEM((1, rows), i32),
            pltpu.VMEM((cap, width), f32),
            pltpu.VMEM((cap, 128), f32),
            pltpu.SMEM((GROUP * seqs,), i32),
            pltpu.SMEM((GROUP * seqs,), i32),
            pltpu.VMEM((2, cap, features), bf16),
            pltpu.VMEM((cap, padded), bf16),
            pltpu.VMEM((cap, units), f32),
            pltpu.VMEM((cap, units), f32),
            pltpu.VMEM((cap, units), f32),
            pltpu.VMEM((cap, max(features, 2 * units)), bf16),
            pltpu.VMEM((cap, 128), f32),
            pltpu.VMEM((cap, 128), f32),
            pltpu.VMEM((2, parts, cap, width), bf16),
            pltpu.VMEM((2, parts, cap, width), bf16),
            pltpu.VMEM((2,) + slots, bf16),
            dma((2 * (units // 128) + 1,)),
            dma((GROUP,)),
            dma((GROUP,)),
            dma((2, 14)),
            dma((2, 14)),
            dma((2, 2, parts)),
            dma((2, 2, parts)),
            dma((2, GROUP)),
            dma((2, GROUP)),
        ],
        compiler_params=pltpu.CompilerParams(
            collective_id=number, has_side_effects=True, vmem_limit_bytes=62 << 20
        ),
        name=f"layer_{cap}",
    )(info, tok, gain, cotangent.reshape(tiled), gate_weight, up_weight, down_weight)


def shards(tokens, gain, gate_weight, up_weight, down_weight, cotangent, lengths):
    tok, info, choice = exchange(tokens, lengths, lax.axis_size("dp"))

    def sized(number, cap):
        return lambda: layer(
            cap, number, info, tok, cotangent, gain, gate_weight, up_weight, down_weight,
            lengths.shape[0],
        )

    out = lax.switch(choice, [sized(i + 1, cap) for i, cap in enumerate(CAPACITIES)])
    return out[0].reshape(tokens.shape), out[1].reshape(tokens.shape)


def solution(mesh):
    placed = (
        P("dp", "tensor"),
        P(),
        P(None, "tensor"),
        P(None, "tensor"),
        P("tensor", None),
        P("dp", "tensor"),
        P("dp"),
    )
    return jax.shard_map(
        shards,
        mesh=mesh,
        in_specs=placed,
        out_specs=(P("dp", "tensor"), P("dp", "tensor")),
        check_vma=False,
    )
```
